256 devices in a mesh: gx: 16 (over z_hi, y, core), gy: 4 (over z_lo), gz: 4 (over x).
Axes of the slice: x: 4, y: 4, z: 8 (z_hi: 2, z_lo: 4; z = z_hi * 4 + z_lo), core: 2. Of those that a mesh axis runs over, the one named last changes fastest.
Arguments:
- offsets: float32 [3, 64, 16, 16, 128], P(None, 'gx', 'gy', 'gz'), may hold values from 0 to 1
- burgers: float32 [3, 64, 16, 16, 128], P(None, 'gx', 'gy', 'gz'), may hold values from -6 to 6
- lines: float32 [3, 64, 16, 16, 128], P(None, 'gx', 'gy', 'gz'), may hold values from -3 to 3
- counts: int32 [64, 16, 16], P('gx', 'gy', 'gz'), may hold values from 1 to 128
- connect: int32 [2, 64, 16, 16, 128], P(None, 'gx', 'gy', 'gz'), may hold values from 0 to 8191
- node_pos: float32 [3, 16, 4, 4, 8192], P(None, 'gx', 'gy', 'gz'), may hold values from -6 to 6
- drag: float32 [16, 4, 4, 8192], P('gx', 'gy', 'gz'), may hold values from 0.5 to 4
- stress: float32 [3, 3], replicated, may hold values from -1 to 1
- shifts: int32 [2, 16, 4, 4], replicated, may hold values from 0 to 512, as said below
Outputs:
- migrated: float32 [6, 16, 4, 4, 9216], P(None, 'gx', 'gy', 'gz')
The draws below stay inside these ranges and needn't reach their ends.
Inputs may be any that keep to these rules, and one draw needn't show every extreme that they name: shifts[0] of the last domain along gx is 0 and shifts[1] of the first is 0; 512 is reached by both rows in every draw.
All inputs are finite; a program needn't handle non-finite values.
Results may differ from the reference program's by a relative error of at most 0.0003.
Values sent between devices are 32-bit elements; how exact they have to be, the bound alone decides.
No kernel may reach another device: no remote copies, remote signals or barrier semaphores. Data moves between devices by JAX's collectives and lax.ppermute only.
A program may use at most 64 MiB of HBM per device.

```python
import math
import jax
import jax.numpy as jnp
from jax import lax

SEGS = 128
CX = 4
CY = 4
CZ = 4
NODES = 8192
MIG = 512
CAP = 9216
NX = 64
NY = 16
NZ = 16
N_GX = 16
N_GY = 4
N_GZ = 4


def draw_shifts(key, part):
    first_key, second_key = jax.random.split(jax.random.fold_in(key, 17))
    upward = jax.random.randint(first_key, (N_GX, N_GY, N_GZ), 0, MIG + 1)
    downward = jax.random.randint(second_key, (N_GX, N_GY, N_GZ), 0, MIG + 1)
    slab_index = lax.broadcasted_iota(jnp.int32, (N_GX, N_GY, N_GZ), 0)
    upward = jnp.where(slab_index == N_GX - 1, 0, upward)
    downward = jnp.where(slab_index == 0, 0, downward)
    upward = upward.at[0, 0, 0].set(MIG)
    downward = downward.at[N_GX - 1, 0, 0].set(MIG)
    return jnp.stack([upward, downward]).astype(jnp.int32)


def place_ends(array, rng, least, high):
    index_at = [jax.random.randint(jax.random.fold_in(rng, axis), (), 0, length) for axis, length in enumerate(array.shape)]
    longest = array.shape.index(max(array.shape))
    neighbour = index_at[:longest] + [(index_at[longest] + 1) % array.shape[longest]] + index_at[longest + 1:]
    return array.at[tuple(index_at)].set(least).at[tuple(neighbour)].set(high)


def shard_levels(own_key, dims, cuts, smallest, largest):
    gain = 1.0
    for axis_at, parts in cuts:
        heights = jax.random.uniform(jax.random.fold_in(jax.random.fold_in(own_key, 6), axis_at), (parts,), jnp.float32, smallest / len(cuts), largest / len(cuts))
        gain = gain * jnp.repeat(jnp.exp(heights), dims[axis_at] // parts).reshape((-1,) + (1,) * (len(dims) - 1 - axis_at))
    return gain


def noise(key, dims, width, reach, shards=(), kind=jnp.bfloat16):
    result = jax.random.normal(key, dims, jnp.float32) * width
    if len(shards) > 0:
        result = shard_levels(key, dims, shards, -0.22, 0.18) * result
    return jnp.clip(result, min=-reach, max=reach).astype(kind)


def setup_inputs(seed: int = 0) -> dict:
    arg_keys = jax.random.split(jax.random.key(seed), 10)
    offsets = jnp.clip(1.0 * jax.random.uniform(arg_keys[0], (3, NX, NY, NZ, SEGS), jnp.float32) ** shard_levels(arg_keys[0], (3, NX, NY, NZ, SEGS), ((1, 16), (2, 4), (3, 4)), -0.2, 0.2), 0.0, 1.0)
    burgers = noise(arg_keys[1], (3, NX, NY, NZ, SEGS), 1.0, 6.0, ((1, 16), (2, 4), (3, 4)), jnp.float32)
    lines = noise(arg_keys[2], (3, NX, NY, NZ, SEGS), 0.5, 3.0, ((1, 16), (2, 4), (3, 4)), jnp.float32)
    counts = place_ends(jax.random.randint(arg_keys[3], (NX, NY, NZ), 1, SEGS + 1), jax.random.fold_in(arg_keys[3], 1), 1, SEGS).astype(jnp.int32)
    connect = place_ends(jax.random.randint(arg_keys[4], (2, NX, NY, NZ, SEGS), 0, NODES), jax.random.fold_in(arg_keys[4], 1), 0, NODES - 1).astype(jnp.int32)
    node_pos = noise(arg_keys[5], (3, N_GX, N_GY, N_GZ, NODES), 1.0, 6.0, ((1, 16), (2, 4), (3, 4)), jnp.float32)
    drag = jnp.clip(jnp.exp(math.log(4.0) - 2.0794415 * jax.random.uniform(arg_keys[6], (N_GX, N_GY, N_GZ, NODES), jnp.float32) ** shard_levels(arg_keys[6], (N_GX, N_GY, N_GZ, NODES), ((0, 16), (1, 4), (2, 4)), -0.2, 0.2)), 0.5, 4.0)
    stress = jnp.clip(jax.random.uniform(arg_keys[7], (3, 3), jnp.float32, -1.0, 1.0), -1.0, 1.0)
    shifts = draw_shifts(jax.random.fold_in(arg_keys[9], 71), 0)
    return {"offsets": offsets, "burgers": burgers, "lines": lines, "counts": counts, "connect": connect, "node_pos": node_pos, "drag": drag, "stress": stress, "shifts": shifts}


SOFTEN_NEAR = 0.25
SOFTEN_FAR = 4.0
NEAR_SCALE = 0.0625
FAR_SCALE = 0.03125
TIME_STEP = 0.1
NEIGHBOURS = ((0, 0, 0), (1, 0, 0), (-1, 0, 0), (0, 1, 0), (0, -1, 0), (0, 0, 1), (0, 0, -1))

def as_index(value):
    return jnp.asarray(value).astype(jnp.int32)

def pair_term(target, source, offset):
    deltas = [target[axis_id][..., :, None] - source[axis_id][..., None, :] - float(offset[axis_id]) for axis_id in range(3)]
    radius = deltas[0] * deltas[0] + deltas[1] * deltas[1] + deltas[2] * deltas[2] + SOFTEN_NEAR
    inverse = lax.rsqrt(radius)
    burgers_dot = target[3][..., :, None] * source[3][..., None, :] + target[4][..., :, None] * source[4][..., None, :] + target[5][..., :, None] * source[5][..., None, :]
    line_dot = target[6][..., :, None] * source[6][..., None, :] + target[7][..., :, None] * source[7][..., None, :] + target[8][..., :, None] * source[8][..., None, :]
    weight = burgers_dot * line_dot * inverse * inverse * inverse
    return jnp.stack([lax.optimization_barrier(jnp.sum(weight * deltas[axis_id], axis=-1)) for axis_id in range(3)])

def far_stress(moments, centers, cells):
    distance = SOFTEN_FAR + jnp.zeros((cells.shape[1], centers.shape[1]), jnp.float32)
    for axis_id in range(3):
        gap = cells[axis_id][:, None] - centers[axis_id][None, :]
        distance = distance + gap * gap
    weights = lax.rsqrt(distance)
    return jnp.dot(moments, weights.T, precision=lax.Precision.HIGHEST, preferred_element_type=jnp.float32)

def segment_force(target, sigma):
    burgers = target[3:6]
    line = target[6:9]
    pulled = [sigma[row, 0][..., None] * burgers[0] + sigma[row, 1][..., None] * burgers[1] + sigma[row, 2][..., None] * burgers[2] for row in range(3)]
    return jnp.stack([pulled[1] * line[2] - pulled[2] * line[1], pulled[2] * line[0] - pulled[0] * line[2], pulled[0] * line[1] - pulled[1] * line[0]])

def coarse_moments(stacked):
    product = jnp.einsum('axyzk,bxyzk->abxyz', stacked[3:6], stacked[6:9], precision=lax.Precision.HIGHEST)
    sx, sy, sz = (product.shape[2], product.shape[3], product.shape[4])
    return product.reshape(9, sx // 2, 2, sy // 2, 2, sz // 2, 2).sum(axis=(2, 4, 6))

def migrate_index(up_prev, down_own, up_own, down_next, nodes, margin, capacity):
    position = lax.broadcasted_iota(jnp.int32, up_prev.shape + (capacity,), len(up_prev.shape))
    upper_in = up_prev[..., None]
    kept = (nodes - up_own - down_own)[..., None]
    source = jnp.where(position < upper_in, margin - upper_in + position, jnp.where(position < upper_in + kept, margin + down_own[..., None] + position - upper_in, margin + nodes + position - upper_in - kept))
    live = position < upper_in + kept + down_next[..., None]
    return (jnp.clip(source, 0, capacity - 1).astype(jnp.int32), live)

def reference(offsets, burgers, lines, counts, connect, node_pos, drag, stress, shifts):
    mask = (lax.broadcasted_iota(jnp.int32, (NX, NY, NZ, SEGS), 3) < counts[..., None]).astype(jnp.float32)
    stacked = jnp.concatenate([offsets, burgers * mask[None], lines], axis=0)
    padded = jnp.pad(stacked, ((0, 0), (1, 1), (1, 1), (1, 1), (0, 0)))
    moments = coarse_moments(stacked).reshape(9, -1)
    coarse_grid = (NX // 2, NY // 2, NZ // 2)
    centers = jnp.stack([(2 * lax.broadcasted_iota(jnp.int32, coarse_grid, axis_id) + 1).astype(jnp.float32).reshape(-1) for axis_id in range(3)])
    zero = as_index(0)

    def plane(index):
        index = as_index(index)
        target = lax.dynamic_slice(stacked, (zero, index, zero, zero, zero), (9, 1, NY, NZ, SEGS))
        near = jnp.zeros((3, 1, NY, NZ, SEGS), jnp.float32)
        for offset in NEIGHBOURS:
            starts = (zero, as_index(index + 1 + offset[0]), as_index(1 + offset[1]), as_index(1 + offset[2]), zero)
            source = lax.dynamic_slice(padded, starts, (9, 1, NY, NZ, SEGS))
            near = near + pair_term(target, source, offset)
        cell_x = jnp.zeros((NY, NZ), jnp.float32) + index.astype(jnp.float32) + 0.5
        cell_y = lax.broadcasted_iota(jnp.int32, (NY, NZ), 0).astype(jnp.float32) + 0.5
        cell_z = lax.broadcasted_iota(jnp.int32, (NY, NZ), 1).astype(jnp.float32) + 0.5
        cells = jnp.stack([cell_x.reshape(-1), cell_y.reshape(-1), cell_z.reshape(-1)])
        sigma = FAR_SCALE * far_stress(moments, centers, cells).reshape(3, 3, 1, NY, NZ) + stress[:, :, None, None, None]
        return NEAR_SCALE * near + segment_force(target, sigma)
    planes = lax.map(plane, jnp.arange(NX, dtype=jnp.int32))
    total = jnp.moveaxis(planes[:, :, 0], 0, 1)
    domain_x = lax.broadcasted_iota(jnp.int32, (NX, NY, NZ), 0) // CX
    domain_y = lax.broadcasted_iota(jnp.int32, (NX, NY, NZ), 1) // CY
    domain_z = lax.broadcasted_iota(jnp.int32, (NX, NY, NZ), 2) // CZ
    domain = (domain_x * N_GY + domain_y) * N_GZ + domain_z
    global_ids = (connect + (domain * NODES)[None, :, :, :, None]).astype(jnp.int32)
    halves = 0.5 * total.reshape(3, -1)
    values = jnp.concatenate([halves, halves], axis=1).T
    node_count = N_GX * N_GY * N_GZ * NODES
    node_force = jax.ops.segment_sum(values, global_ids.reshape(-1), num_segments=node_count).T
    node_force = node_force.reshape(3, N_GX, N_GY, N_GZ, NODES)
    velocity = node_force / drag[None]
    fields = jnp.concatenate([node_pos + TIME_STEP * velocity, velocity], axis=0)
    empty = jnp.zeros((6, 1, N_GY, N_GZ, MIG), jnp.float32)
    from_below = jnp.concatenate([empty, fields[:, :-1, :, :, NODES - MIG:]], axis=1)
    from_above = jnp.concatenate([fields[:, 1:, :, :, :MIG], empty], axis=1)
    sectioning = jnp.concatenate([from_below, fields, from_above], axis=4)
    zero_row = jnp.zeros((1, N_GY, N_GZ), jnp.int32)
    up_own = shifts[0]
    down_own = shifts[1]
    up_prev = jnp.concatenate([zero_row, up_own[:-1]], axis=0)
    down_next = jnp.concatenate([down_own[1:], zero_row], axis=0)
    source, live = migrate_index(up_prev, down_own, up_own, down_next, NODES, MIG, CAP)
    picked = jnp.take_along_axis(sectioning, jnp.broadcast_to(source[None], sectioning.shape), axis=4)
    return jnp.where(live[None], picked, 0.0)
```

```python
import functools
import jax
import jax.numpy as jnp
from jax import lax
from jax.experimental import pallas as pl
from jax.experimental.pallas import tpu as pltpu
from jax.sharding import PartitionSpec as P

SOFTEN_NEAR = 0.25
SOFTEN_FAR = 4.0
NEAR_SCALE = 0.0625
FAR_SCALE = 0.03125
TIME_STEP = 0.1
AXES = ("gx", "gy", "gz")
F32 = jnp.float32
BF16 = jnp.bfloat16
LANES = 128
CELLS = 64
FACE = 16
SOURCES = CELLS + 6 * FACE
FACES = ("xlo", "xhi", "ylo", "yhi", "zlo", "zhi")
VMEM = 60 << 20


def face_rows(name):
    return {
        "xlo": [(0, 16, 1)],
        "xhi": [(48, 16, 1)],
        "ylo": [(16 * x, 4, 1) for x in range(4)],
        "yhi": [(16 * x + 12, 4, 1) for x in range(4)],
        "zlo": [(0, 16, 4)],
        "zhi": [(3, 16, 4)],
    }[name]


def split3(value):
    high = value.astype(BF16).astype(F32)
    rest = value - high
    middle = rest.astype(BF16).astype(F32)
    return high, middle, rest - middle


def prepare_kernel(offsets, burgers, lines, counts, masked, moments, *faces):
    slot = lax.broadcasted_iota(jnp.int32, (8, LANES), 1)
    row = lax.broadcasted_iota(jnp.int32, (8, LANES), 0)
    for group in range(8):
        live = jnp.zeros((8, LANES), jnp.int32)
        for s in range(8):
            cell = 8 * group + s
            live = jnp.where(row == s, counts[cell // 16, (cell // 4) % 4, cell % 4], live)
        for axis in range(3):
            block = burgers[axis, pl.ds(8 * group, 8), :]
            masked[axis, pl.ds(8 * group, 8), :] = jnp.where(slot < live, block, 0.0)
    for name, face in zip(FACES, faces):
        to = 0
        for start, size, stride in face_rows(name):
            at = pl.ds(start, size, stride=stride) if stride > 1 else pl.ds(start, size)
            for axis in range(3):
                face[axis, pl.ds(to, size), :] = offsets[axis, at, :]
                face[3 + axis, pl.ds(to, size), :] = masked[axis, at, :]
                face[6 + axis, pl.ds(to, size), :] = lines[axis, at, :]
            to += size
    rows = []
    for coarse in range(4):
        big_x, big_y = coarse // 2, coarse % 2
        groups = (4 * big_x + big_y, 4 * big_x + 2 + big_y)
        for a in range(3):
            for b in range(3):
                rows.append(
                    sum(
                        masked[a, pl.ds(8 * g, 8), :] * lines[b, pl.ds(8 * g, 8), :]
                        for g in groups
                    )
                )
    stack = jnp.concatenate(rows, axis=0)
    ones = jnp.ones((8, LANES), F32)
    summed = lax.dot_general(
        ones,
        stack,
        (((1,), (1,)), ((), ())),
        precision=lax.Precision.HIGHEST,
        preferred_element_type=F32,
    )
    n = lax.broadcasted_iota(jnp.int32, (288, LANES), 0)
    lane = lax.broadcasted_iota(jnp.int32, (288, LANES), 1)
    target = ((n // 72) * 2 + (n % 4) // 2) * 16 + (n // 8) % 9
    pick = (lane == target).astype(F32)
    packed = jnp.dot(summed, pick, precision=lax.Precision.HIGHEST, preferred_element_type=F32)
    moments[...] = jnp.broadcast_to(packed[0:1], moments.shape)


def source_index(target):
    x, y, z = target >> 4, (target >> 2) & 3, target & 3
    first = CELLS
    return [
        target,
        jnp.where(x > 0, target - 16, first + (target & 15)),
        jnp.where(x < 3, target + 16, first + 16 + (target & 15)),
        jnp.where(y > 0, target - 4, first + 32 + x * 4 + z),
        jnp.where(y < 3, target + 4, first + 48 + x * 4 + z),
        jnp.where(z > 0, target - 1, first + 64 + (target >> 2)),
        jnp.where(z < 3, target + 1, first + 80 + (target >> 2)),
    ]


PAIRS = ((0, 0), (0, 1), (1, 0), (0, 2), (2, 0), (1, 1))


def near_kernel(*refs):
    offsets, masked, lines = refs[:3]
    faces = refs[3:9]
    near = refs[9]
    rows_s, rows_t, source, target, points = refs[10:]
    blocks = []
    for first in range(0, CELLS, 16):
        cell = first + lax.broadcasted_iota(jnp.int32, (16, LANES), 0)
        corner = (cell // 16, (cell // 4) % 4, cell % 4)
        blocks.append(
            (
                first,
                [offsets[a, pl.ds(first, 16), :] + (corner[a].astype(F32) - 2.0) for a in range(3)],
                [masked[a, pl.ds(first, 16), :] for a in range(3)],
                [lines[a, pl.ds(first, 16), :] for a in range(3)],
            )
        )
    cell = lax.broadcasted_iota(jnp.int32, (16, LANES), 0)
    for f, face in enumerate(faces):
        fixed = f // 2
        others = [a for a in range(3) if a != fixed]
        corner = [None] * 3
        corner[fixed] = -3.0 if f % 2 == 0 else 2.0
        corner[others[0]] = (cell // 4).astype(F32) - 2.0
        corner[others[1]] = (cell % 4).astype(F32) - 2.0
        blocks.append(
            (
                CELLS + FACE * f,
                [face[a] + corner[a] for a in range(3)],
                [face[3 + a] for a in range(3)],
                [face[6 + a] for a in range(3)],
            )
        )
    one = jnp.ones((16, LANES), F32)
    zero = jnp.zeros((16, LANES), F32)
    rows_s[:, pl.ds(80, 48), :] = jnp.zeros((SOURCES, 48, LANES), F32)
    rows_t[:, pl.ds(80, 48), :] = jnp.zeros((CELLS, 48, LANES), F32)
    for first, place, burger, line in blocks:
        own = first < CELLS
        place_parts = [split3(p) for p in place]
        norm = split3(place[0] * place[0] + place[1] * place[1] + place[2] * place[2])
        outer = [split3(burger[a] * line[b]) for a in range(3) for b in range(3)]
        k = 0
        for s, t in PAIRS:
            for a in range(3):
                rows_s[pl.ds(first, 16), k, :] = place_parts[a][s]
                if own:
                    rows_t[pl.ds(first, 16), k, :] = -2.0 * place_parts[a][t]
                k += 1
        if own:
            shifted = split3(
                place[0] * place[0] + place[1] * place[1] + place[2] * place[2] + SOFTEN_NEAR
            )
        for s in range(3):
            rows_s[pl.ds(first, 16), k, :] = norm[s]
            if own:
                rows_t[pl.ds(first, 16), k, :] = one
            k += 1
        for s in range(3):
            rows_s[pl.ds(first, 16), k, :] = one
            if own:
                rows_t[pl.ds(first, 16), k, :] = shifted[s]
            k += 1
        for s, t in PAIRS:
            for ab in range(9):
                rows_s[pl.ds(first, 16), k, :] = outer[ab][s]
                if own:
                    rows_t[pl.ds(first, 16), k, :] = outer[ab][t]
                k += 1
        for k in (78, 79):
            rows_s[pl.ds(first, 16), k, :] = zero
            if own:
                rows_t[pl.ds(first, 16), k, :] = zero

    def arrange(c, carry):
        block = rows_s[c]
        source[c] = block.T.astype(BF16)
        head = block[0:24]
        points[c] = jnp.concatenate(
            [head[0:3], head[6:9], head[12:15], head[21:22], jnp.zeros((6, LANES), F32)], axis=0
        ).astype(BF16)
        return carry

    lax.fori_loop(0, SOURCES, arrange, 0)

    def arrange_target(c, carry):
        block = rows_t[c]
        row = lax.broadcasted_iota(jnp.int32, (LANES, LANES), 0)
        target[c, :, :LANES] = jnp.where(row < 24, block, 0.0).astype(BF16)
        target[c, :, LANES:] = jnp.where(row < 24, 0.0, block).astype(BF16)
        return carry

    lax.fori_loop(0, CELLS, arrange_target, 0)
    together = 2

    def step(i, carry):
        cells = [i * together + u for u in range(together)]
        sources = [source_index(c) for c in cells]
        stationary = [target[c] for c in cells]
        weights = [[] for _ in cells]
        spots = [[] for _ in cells]
        for k in range(7):
            for u in range(together):
                pair = jnp.dot(source[sources[u][k]], stationary[u], preferred_element_type=F32)
                inverse = lax.rsqrt(pair[:, :LANES])
                weight = pair[:, LANES:] * (inverse * inverse * inverse)
                high = weight.astype(BF16)
                low = (weight - high.astype(F32)).astype(BF16)
                weights[u].append(jnp.concatenate([high, low], axis=1))
                spots[u].append(points[sources[u][k]])
        for u in range(together):
            both = jnp.dot(
                jnp.concatenate(spots[u], axis=1),
                jnp.concatenate(weights[u], axis=0),
                preferred_element_type=F32,
            )
            sums = both[:, :LANES] + both[:, LANES:]
            moved = sums[0:3] + sums[3:6] + sums[6:9]
            total = sums[9:10]
            base = rows_t[cells[u], 0:24, :]
            place = -0.5 * (base[0:3] + base[3:6] + base[9:12])
            near[cells[u]] = place * total - moved
        return carry

    lax.fori_loop(0, CELLS // together, step, 0)


def node_kernel(
    gathered, near, masked, lines, stress, connect, node_pos, drag, fields, tail, head,
    values, sums, left, right,
):
    index_x, index_y, index_z = (lax.axis_index(a) for a in AXES)
    device = lax.broadcasted_iota(jnp.int32, (CELLS, 256), 1)
    cell = lax.broadcasted_iota(jnp.int32, (CELLS, 256), 0)
    gap = [
        (4 * index_x + cell // 16 - 4 * (device // 16)).astype(F32) - 0.5,
        (4 * index_y + (cell // 4) % 4 - 4 * ((device // 4) % 4)).astype(F32) - 0.5,
        (4 * index_z + cell % 4 - 4 * (device % 4)).astype(F32) - 0.5,
    ]
    square = [[gap[a] * gap[a], (gap[a] - 2.0) * (gap[a] - 2.0)] for a in range(3)]
    moments = gathered[...]
    lane = lax.broadcasted_iota(jnp.int32, (CELLS, LANES), 1)
    sigma = jnp.zeros((CELLS, LANES), F32)
    for sub in range(8):
        big_x, big_y, big_z = sub // 4, (sub // 2) % 2, sub % 2
        weight = lax.rsqrt(square[0][big_x] + square[1][big_y] + square[2][big_z] + SOFTEN_FAR)
        part = jnp.dot(
            weight, moments, precision=lax.Precision.HIGHEST, preferred_element_type=F32
        )
        sigma = jnp.where(lane // 16 == sub, part, sigma)
    for shift in (64, 32, 16):
        sigma = sigma + pltpu.roll(sigma, shift, 1)
    pull = [
        [FAR_SCALE * sigma[:, 3 * a + b : 3 * a + b + 1] + stress[a, b] for b in range(3)]
        for a in range(3)
    ]
    burger = [masked[a] for a in range(3)]
    line = [lines[a] for a in range(3)]
    pulled = [
        pull[a][0] * burger[0] + pull[a][1] * burger[1] + pull[a][2] * burger[2] for a in range(3)
    ]
    for a in range(3):
        b, c = (a + 1) % 3, (a + 2) % 3
        force = NEAR_SCALE * near[:, a, :] + (pulled[b] * line[c] - pulled[c] * line[b])
        parts = split3(0.5 * force)
        for p in range(3):
            values[3 * p + a] = parts[p]
    sums[...] = jnp.zeros(sums.shape, F32)
    rows_high = lax.broadcasted_iota(jnp.int32, (32, LANES), 0)
    rows_low = lax.broadcasted_iota(jnp.int32, (256, LANES), 0)
    step_cells = 4

    def scatter(i, carry):
        for u in range(step_cells):
            at = i * step_cells + u
            for end in range(2):
                column = (2 * u + end) * LANES
                node = connect[end, pl.ds(at, 1), :]
                chosen = rows_high == (node >> 8)
                for q in range(9):
                    left[pl.ds(32 * q, 32), pl.ds(column, LANES)] = jnp.where(
                        chosen, values[q, pl.ds(at, 1), :], 0.0
                    ).astype(BF16)
                right[:, pl.ds(column, LANES)] = (
                    (rows_low == (node & 255)).astype(F32).astype(BF16)
                )
        sums[...] += lax.dot_general(
            left[...], right[...], (((1,), (1,)), ((), ())), preferred_element_type=F32
        )
        return carry

    lax.fori_loop(0, CELLS // step_cells, scatter, 0)
    for a in range(3):
        force = (
            sums[pl.ds(32 * a, 32), :]
            + sums[pl.ds(96 + 32 * a, 32), :]
            + sums[pl.ds(192 + 32 * a, 32), :]
        )
        fields[3 + a, pl.ds(0, 32, stride=2), :] = force[:, :LANES]
        fields[3 + a, pl.ds(1, 32, stride=2), :] = force[:, LANES:]
    for a in range(3):
        velocity = fields[3 + a] / drag[...]
        fields[3 + a] = velocity
        fields[a] = node_pos[a] + TIME_STEP * velocity
    for a in range(6):
        tail[a] = fields[a, pl.ds(60, 4), :]
        head[a] = fields[a, pl.ds(0, 4), :]


def migrate_kernel(fields, below, above, shifts, out, joined):
    index_x, index_y, index_z = (lax.axis_index(a) for a in AXES)
    last = lax.axis_size("gx") - 1
    up_own = shifts[0, index_y, index_z, index_x]
    down_own = shifts[1, index_y, index_z, index_x]
    up_prev = jnp.where(
        index_x > 0, shifts[0, index_y, index_z, jnp.maximum(index_x - 1, 0)], 0
    )
    down_next = jnp.where(
        index_x < last, shifts[1, index_y, index_z, jnp.minimum(index_x + 1, last)], 0
    )
    kept = 8192 - up_own - down_own
    row = lax.broadcasted_iota(jnp.int32, (72, LANES), 0)
    lane = lax.broadcasted_iota(jnp.int32, (72, LANES), 1)
    position = row * LANES + lane
    pieces = (
        (512 - up_prev, position < up_prev),
        (512 + down_own - up_prev, position < up_prev + kept),
        (8704 - up_prev - kept, position < up_prev + kept + down_next),
    )
    for a in range(6):
        joined[pl.ds(0, 4), :] = below[a]
        joined[pl.ds(4, 64), :] = fields[a]
        joined[pl.ds(68, 4), :] = above[a]
        result = jnp.zeros((72, LANES), F32)
        for delta, within in reversed(pieces):
            rows, lanes = delta >> 7, delta & 127
            first = pltpu.roll(joined[pl.ds(rows, 72), :], (LANES - lanes) & 127, 1)
            second = pltpu.roll(joined[pl.ds(rows + 1, 72), :], (LANES - lanes) & 127, 1)
            moved = jnp.where(lane < LANES - lanes, first, second)
            result = jnp.where(within, moved, result)
        out[a] = result


def passed_along(array, axis, by):
    count = lax.axis_size(axis)
    pairs = [(i, i + by) for i in range(count) if 0 <= i + by < count]
    return lax.ppermute(array, axis, pairs)


def shape(*dims, dtype=F32):
    return jax.ShapeDtypeStruct(dims, dtype)


def shards(offsets, burgers, lines, counts, connect, node_pos, drag, stress, shifts):
    offsets = offsets.reshape(3, CELLS, LANES)
    burgers = burgers.reshape(3, CELLS, LANES)
    lines = lines.reshape(3, CELLS, LANES)
    connect = connect.reshape(2, CELLS, LANES)
    node_pos = node_pos.reshape(3, 64, LANES)
    drag = drag.reshape(64, LANES)
    shifts = shifts.transpose(0, 2, 3, 1)
    vmem = pl.BlockSpec(memory_space=pltpu.VMEM)
    smem = pl.BlockSpec(memory_space=pltpu.SMEM)
    params = pltpu.CompilerParams(vmem_limit_bytes=VMEM)
    masked, moments, *faces = pl.pallas_call(
        prepare_kernel,
        in_specs=[vmem, vmem, vmem, smem],
        out_shape=[shape(3, CELLS, LANES), shape(256, LANES)] + [shape(9, FACE, LANES)] * 6,
        compiler_params=params,
        name="prepare",
    )(offsets, burgers, lines, counts)
    by_name = dict(zip(FACES, faces))
    received = []
    for axis, name in zip(AXES, "xyz"):
        received.append(passed_along(by_name[name + "hi"], axis, 1))
        received.append(passed_along(by_name[name + "lo"], axis, -1))
    gathered = lax.all_to_all(
        moments.reshape(256, 1, LANES), AXES, 0, 0, tiled=True
    ).reshape(256, LANES)
    near = pl.pallas_call(
        near_kernel,
        in_specs=[vmem] * 9,
        out_shape=shape(CELLS, 3, LANES),
        scratch_shapes=[
            pltpu.VMEM((SOURCES, LANES, LANES), F32),
            pltpu.VMEM((CELLS, LANES, LANES), F32),
            pltpu.VMEM((SOURCES, LANES, LANES), BF16),
            pltpu.VMEM((CELLS, LANES, 2 * LANES), BF16),
            pltpu.VMEM((SOURCES, 16, LANES), BF16),
        ],
        compiler_params=params,
        name="near",
    )(offsets, masked, lines, *received)
    fields, tail, head = pl.pallas_call(
        node_kernel,
        in_specs=[vmem] * 4 + [smem] + [vmem] * 3,
        out_shape=[shape(6, 64, LANES), shape(6, 4, LANES), shape(6, 4, LANES)],
        scratch_shapes=[
            pltpu.VMEM((9, CELLS, LANES), F32),
            pltpu.VMEM((288, 256), F32),
            pltpu.VMEM((288, 1024), BF16),
            pltpu.VMEM((256, 1024), BF16),
        ],
        compiler_params=params,
        name="nodes",
    )(gathered, near, masked, lines, stress, connect, node_pos, drag)
    below = passed_along(tail, "gx", 1)
    above = passed_along(head, "gx", -1)
    out = pl.pallas_call(
        migrate_kernel,
        in_specs=[vmem] * 3 + [smem],
        out_shape=shape(6, 72, LANES),
        scratch_shapes=[pltpu.VMEM((96, LANES), F32)],
        compiler_params=params,
        name="migrate",
    )(fields, below, above, shifts)
    return out.reshape(6, 1, 1, 1, 72 * LANES)


def solution(mesh):
    cells = P(None, "gx", "gy", "gz", None)
    return jax.shard_map(
        shards,
        mesh=mesh,
        in_specs=(cells, cells, cells, P("gx", "gy", "gz"), cells, cells,
                  P("gx", "gy", "gz", None), P(), P()),
        out_specs=cells,
        check_vma=False,
    )
```

```python
import functools
import jax
import jax.numpy as jnp
from jax import lax
from jax.experimental import pallas as pl
from jax.experimental.pallas import tpu as pltpu
from jax.sharding import PartitionSpec as P

SOFTEN_NEAR = 0.25
SOFTEN_FAR = 4.0
NEAR_SCALE = 0.0625
FAR_SCALE = 0.03125
TIME_STEP = 0.1
AXES = ("gx", "gy", "gz")
F32 = jnp.float32
BF16 = jnp.bfloat16
LANES = 128
DEPTH = 64
CELLS = 64
FACE = 16
SOURCES = CELLS + 6 * FACE
VMEM = 60 << 20


def face_rows(axis):
    return (
        [(0, 48, 16, 1)],
        [(16 * x, 16 * x + 12, 4, 1) for x in range(4)],
        [(0, 3, 16, 4)],
    )[axis]


def split3(value):
    high = value.astype(BF16).astype(F32)
    rest = value - high
    middle = rest.astype(BF16).astype(F32)
    return high, middle, rest - middle


def prepare_kernel(offsets, burgers, lines, counts, masked, *sends):
    slot = lax.broadcasted_iota(jnp.int32, (8, LANES), 1)
    row = lax.broadcasted_iota(jnp.int32, (8, LANES), 0)
    for group in range(8):
        live = jnp.zeros((8, LANES), jnp.int32)
        for s in range(8):
            cell = 8 * group + s
            live = jnp.where(row == s, counts[cell // 16, (cell // 4) % 4, cell % 4], live)
        for axis in range(3):
            block = burgers[axis, pl.ds(8 * group, 8), :]
            masked[axis, pl.ds(8 * group, 8), :] = jnp.where(slot < live, block, 0.0)
    for axis in range(3):
        even = lax.axis_index(AXES[axis]) % 2 == 0
        to = 0
        for low, high, size, stride in face_rows(axis):
            at_low = pl.ds(low, size, stride=stride) if stride > 1 else pl.ds(low, size)
            at_high = pl.ds(high, size, stride=stride) if stride > 1 else pl.ds(high, size)
            for a in range(3):
                for part, array in enumerate((offsets, masked, lines)):
                    of_low, of_high = array[a, at_low, :], array[a, at_high, :]
                    sends[2 * axis][3 * part + a, pl.ds(to, size), :] = jnp.where(
                        even, of_high, of_low
                    )
                    sends[2 * axis + 1][3 * part + a, pl.ds(to, size), :] = jnp.where(
                        even, of_low, of_high
                    )
            to += size


def moments_kernel(masked, lines, moments):
    rows = []
    for coarse in range(4):
        big_x, big_y = coarse // 2, coarse % 2
        groups = (4 * big_x + big_y, 4 * big_x + 2 + big_y)
        for a in range(3):
            for b in range(3):
                rows.append(
                    sum(
                        masked[a, pl.ds(8 * g, 8), :] * lines[b, pl.ds(8 * g, 8), :]
                        for g in groups
                    )
                )
    stack = jnp.concatenate(rows, axis=0)
    ones = jnp.ones((8, LANES), F32)
    summed = lax.dot_general(
        ones,
        stack,
        (((1,), (1,)), ((), ())),
        precision=lax.Precision.HIGHEST,
        preferred_element_type=F32,
    )
    n = lax.broadcasted_iota(jnp.int32, (288, LANES), 0)
    lane = lax.broadcasted_iota(jnp.int32, (288, LANES), 1)
    target = ((n // 72) * 2 + (n % 4) // 2) * 16 + (n // 8) % 9
    pick = (lane == target).astype(F32)
    packed = jnp.dot(summed, pick, precision=lax.Precision.HIGHEST, preferred_element_type=F32)
    moments[...] = jnp.broadcast_to(packed[0:1], moments.shape)


def source_index(target):
    x, y, z = target >> 4, (target >> 2) & 3, target & 3
    odd = [lax.axis_index(a) & 1 for a in AXES]
    upper = [CELLS + 2 * FACE * a + FACE * odd[a] for a in range(3)]
    lower = [CELLS + 2 * FACE * a + FACE * (1 - odd[a]) for a in range(3)]
    return [
        target,
        jnp.where(x > 0, target - 16, lower[0] + (target & 15)),
        jnp.where(x < 3, target + 16, upper[0] + (target & 15)),
        jnp.where(y > 0, target - 4, lower[1] + x * 4 + z),
        jnp.where(y < 3, target + 4, upper[1] + x * 4 + z),
        jnp.where(z > 0, target - 1, lower[2] + (target >> 2)),
        jnp.where(z < 3, target + 1, upper[2] + (target >> 2)),
    ]


PAIRS = ((0, 0), (0, 1), (1, 0), (0, 2), (2, 0), (1, 1))


def near_kernel(*refs):
    offsets, masked, lines = refs[:3]
    faces = refs[3:9]
    near = refs[9]
    rows_s, rows_t, source, target, points = refs[10:]
    blocks = []
    for first in range(0, CELLS, 16):
        cell = first + lax.broadcasted_iota(jnp.int32, (16, LANES), 0)
        corner = (cell // 16, (cell // 4) % 4, cell % 4)
        blocks.append(
            (
                first,
                [offsets[a, pl.ds(first, 16), :] + (corner[a].astype(F32) - 2.0) for a in range(3)],
                [masked[a, pl.ds(first, 16), :] for a in range(3)],
                [lines[a, pl.ds(first, 16), :] for a in range(3)],
            )
        )
    cell = lax.broadcasted_iota(jnp.int32, (16, LANES), 0)
    for f, face in enumerate(faces):
        fixed = f // 2
        others = [a for a in range(3) if a != fixed]
        corner = [None] * 3
        upper = lax.axis_index(AXES[fixed]) % 2 == f % 2
        corner[fixed] = jnp.where(upper, 2.0, -3.0).astype(F32)
        corner[others[0]] = (cell // 4).astype(F32) - 2.0
        corner[others[1]] = (cell % 4).astype(F32) - 2.0
        blocks.append(
            (
                CELLS + FACE * f,
                [face[a] + corner[a] for a in range(3)],
                [face[3 + a] for a in range(3)],
                [face[6 + a] for a in range(3)],
            )
        )
    one = jnp.ones((16, LANES), F32)
    rows_s[:, pl.ds(48, DEPTH - 48), :] = jnp.zeros((SOURCES, DEPTH - 48, LANES), F32)
    rows_t[:, pl.ds(48, DEPTH - 48), :] = jnp.zeros((CELLS, DEPTH - 48, LANES), F32)
    for first, place, burger, line in blocks:
        own = first < CELLS
        place_parts = [split3(p) for p in place]
        norm = split3(place[0] * place[0] + place[1] * place[1] + place[2] * place[2])
        outer = [split3(burger[a] * line[b]) for a in range(3) for b in range(3)]
        k = 0
        for s, t in PAIRS:
            for a in range(3):
                rows_s[pl.ds(first, 16), k, :] = place_parts[a][s]
                if own:
                    rows_t[pl.ds(first, 16), k, :] = -2.0 * place_parts[a][t]
                k += 1
        if own:
            shifted = split3(
                place[0] * place[0] + place[1] * place[1] + place[2] * place[2] + SOFTEN_NEAR
            )
        for s in range(3):
            rows_s[pl.ds(first, 16), k, :] = norm[s]
            if own:
                rows_t[pl.ds(first, 16), k, :] = one
            k += 1
        for s in range(3):
            rows_s[pl.ds(first, 16), k, :] = one
            if own:
                rows_t[pl.ds(first, 16), k, :] = shifted[s]
            k += 1
        for s, t in PAIRS[:3]:
            for ab in range(9):
                rows_s[pl.ds(first, 16), k, :] = outer[ab][s]
                if own:
                    rows_t[pl.ds(first, 16), k, :] = outer[ab][t]
                k += 1

    def arrange(c, carry):
        block = rows_s[c]
        source[c] = block.astype(BF16).T
        head = block[0:24]
        points[c] = jnp.concatenate(
            [head[0:3], head[6:9], head[12:15], head[21:22], jnp.zeros((6, LANES), F32)], axis=0
        ).astype(BF16)
        return carry

    lax.fori_loop(0, SOURCES, arrange, 0, unroll=8)

    def arrange_target(c, carry):
        block = rows_t[c]
        row = lax.broadcasted_iota(jnp.int32, (DEPTH, LANES), 0)
        target[c, :, :LANES] = jnp.where(row < 24, block, 0.0).astype(BF16)
        target[c, :, LANES:] = jnp.where(row < 24, 0.0, block).astype(BF16)
        return carry

    lax.fori_loop(0, CELLS, arrange_target, 0, unroll=4)
    together = 2

    def step(i, carry):
        cells = [i * together + u for u in range(together)]
        sources = [source_index(c) for c in cells]
        stationary = [target[c] for c in cells]
        weights = [[] for _ in cells]
        spots = [[] for _ in cells]
        for k in range(7):
            for u in range(together):
                pair = jnp.dot(source[sources[u][k]], stationary[u], preferred_element_type=F32)
                inverse = lax.rsqrt(pair[:, :LANES])
                weight = pair[:, LANES:] * (inverse * inverse * inverse)
                high = weight.astype(BF16)
                low = (weight - high.astype(F32)).astype(BF16)
                weights[u].append(jnp.concatenate([high, low], axis=1))
                spots[u].append(points[sources[u][k]])
        for u in range(together):
            both = jnp.dot(
                jnp.concatenate(spots[u], axis=1),
                jnp.concatenate(weights[u], axis=0),
                preferred_element_type=F32,
            )
            sums = both[:, :LANES] + both[:, LANES:]
            moved = sums[0:3] + sums[3:6] + sums[6:9]
            total = sums[9:10]
            base = rows_t[cells[u], 0:24, :]
            place = -0.5 * (base[0:3] + base[3:6] + base[9:12])
            near[cells[u]] = place * total - moved
        return carry

    lax.fori_loop(0, CELLS // together, step, 0)


def node_kernel(
    gathered, near, masked, lines, stress, connect, node_pos, drag, fields, first, second,
    values, sums, left, right,
):
    index_x, index_y, index_z = (lax.axis_index(a) for a in AXES)
    device = lax.broadcasted_iota(jnp.int32, (CELLS, 256), 1)
    cell = lax.broadcasted_iota(jnp.int32, (CELLS, 256), 0)
    gap = [
        (4 * index_x + cell // 16 - 4 * (device // 16)).astype(F32) - 0.5,
        (4 * index_y + (cell // 4) % 4 - 4 * ((device // 4) % 4)).astype(F32) - 0.5,
        (4 * index_z + cell % 4 - 4 * (device % 4)).astype(F32) - 0.5,
    ]
    square = [[gap[a] * gap[a], (gap[a] - 2.0) * (gap[a] - 2.0)] for a in range(3)]
    moments = gathered[...]
    lane = lax.broadcasted_iota(jnp.int32, (CELLS, LANES), 1)
    sigma = jnp.zeros((CELLS, LANES), F32)
    for sub in range(8):
        big_x, big_y, big_z = sub // 4, (sub // 2) % 2, sub % 2
        weight = lax.rsqrt(square[0][big_x] + square[1][big_y] + square[2][big_z] + SOFTEN_FAR)
        part = jnp.dot(
            weight, moments, precision=lax.Precision.HIGHEST, preferred_element_type=F32
        )
        sigma = jnp.where(lane // 16 == sub, part, sigma)
    for shift in (64, 32, 16):
        sigma = sigma + pltpu.roll(sigma, shift, 1)
    pull = [
        [FAR_SCALE * sigma[:, 3 * a + b : 3 * a + b + 1] + stress[a, b] for b in range(3)]
        for a in range(3)
    ]
    burger = [masked[a] for a in range(3)]
    line = [lines[a] for a in range(3)]
    pulled = [
        pull[a][0] * burger[0] + pull[a][1] * burger[1] + pull[a][2] * burger[2] for a in range(3)
    ]
    for a in range(3):
        b, c = (a + 1) % 3, (a + 2) % 3
        force = NEAR_SCALE * near[:, a, :] + (pulled[b] * line[c] - pulled[c] * line[b])
        parts = split3(0.5 * force)
        for p in range(3):
            values[3 * p + a] = parts[p]
    sums[...] = jnp.zeros(sums.shape, F32)
    rows_high = lax.broadcasted_iota(jnp.int32, (32, LANES), 0)
    rows_low = lax.broadcasted_iota(jnp.int32, (256, LANES), 0)
    step_cells = 4

    def scatter(i, carry):
        for u in range(step_cells):
            at = i * step_cells + u
            for end in range(2):
                column = (2 * u + end) * LANES
                node = connect[end, pl.ds(at, 1), :]
                chosen = rows_high == (node >> 8)
                for q in range(9):
                    left[pl.ds(32 * q, 32), pl.ds(column, LANES)] = jnp.where(
                        chosen, values[q, pl.ds(at, 1), :], 0.0
                    ).astype(BF16)
                right[:, pl.ds(column, LANES)] = (
                    (rows_low == (node & 255)).astype(F32).astype(BF16)
                )
        sums[...] += lax.dot_general(
            left[...], right[...], (((1,), (1,)), ((), ())), preferred_element_type=F32
        )
        return carry

    lax.fori_loop(0, CELLS // step_cells, scatter, 0)
    for a in range(3):
        force = (
            sums[pl.ds(32 * a, 32), :]
            + sums[pl.ds(96 + 32 * a, 32), :]
            + sums[pl.ds(192 + 32 * a, 32), :]
        )
        fields[3 + a, pl.ds(0, 32, stride=2), :] = force[:, :LANES]
        fields[3 + a, pl.ds(1, 32, stride=2), :] = force[:, LANES:]
    for a in range(3):
        velocity = fields[3 + a] / drag[...]
        fields[3 + a] = velocity
        fields[a] = node_pos[a] + TIME_STEP * velocity
    even = index_x % 2 == 0
    for a in range(6):
        tail = fields[a, pl.ds(60, 4), :]
        head = fields[a, pl.ds(0, 4), :]
        first[a] = jnp.where(even, tail, head)
        second[a] = jnp.where(even, head, tail)


def migrate_kernel(fields, first, second, shifts, out, joined):
    index_x, index_y, index_z = (lax.axis_index(a) for a in AXES)
    last = lax.axis_size("gx") - 1
    even = index_x % 2 == 0
    up_own = shifts[0, index_y, index_z, index_x]
    down_own = shifts[1, index_y, index_z, index_x]
    up_prev = jnp.where(
        index_x > 0, shifts[0, index_y, index_z, jnp.maximum(index_x - 1, 0)], 0
    )
    down_next = jnp.where(
        index_x < last, shifts[1, index_y, index_z, jnp.minimum(index_x + 1, last)], 0
    )
    kept = 8192 - up_own - down_own
    row = lax.broadcasted_iota(jnp.int32, (72, LANES), 0)
    lane = lax.broadcasted_iota(jnp.int32, (72, LANES), 1)
    position = row * LANES + lane
    pieces = (
        (512 - up_prev, position < up_prev),
        (512 + down_own - up_prev, position < up_prev + kept),
        (8704 - up_prev - kept, position < up_prev + kept + down_next),
    )
    for a in range(6):
        joined[pl.ds(0, 4), :] = jnp.where(even, second[a], first[a])
        joined[pl.ds(4, 64), :] = fields[a]
        joined[pl.ds(68, 4), :] = jnp.where(even, first[a], second[a])
        result = jnp.zeros((72, LANES), F32)
        for delta, within in reversed(pieces):
            rows, lanes = delta >> 7, delta & 127
            here = pltpu.roll(joined[pl.ds(rows, 72), :], (LANES - lanes) & 127, 1)
            after = pltpu.roll(joined[pl.ds(rows + 1, 72), :], (LANES - lanes) & 127, 1)
            moved = jnp.where(lane < LANES - lanes, here, after)
            result = jnp.where(within, moved, result)
        out[a] = result


def exchanged(array, axis, first):
    pairs = [(i, i + 1) for i in range(first, lax.axis_size(axis) - 1, 2)]
    return lax.ppermute(array, axis, pairs + [(b, a) for a, b in pairs])


def shape(*dims, dtype=F32):
    return jax.ShapeDtypeStruct(dims, dtype)


def shards(offsets, burgers, lines, counts, connect, node_pos, drag, stress, shifts):
    offsets = offsets.reshape(3, CELLS, LANES)
    burgers = burgers.reshape(3, CELLS, LANES)
    lines = lines.reshape(3, CELLS, LANES)
    connect = connect.reshape(2, CELLS, LANES)
    node_pos = node_pos.reshape(3, 64, LANES)
    drag = drag.reshape(64, LANES)
    shifts = shifts.transpose(0, 2, 3, 1)
    vmem = pl.BlockSpec(memory_space=pltpu.VMEM)
    smem = pl.BlockSpec(memory_space=pltpu.SMEM)
    params = pltpu.CompilerParams(vmem_limit_bytes=VMEM)
    masked, *sends = pl.pallas_call(
        prepare_kernel,
        in_specs=[vmem, vmem, vmem, smem],
        out_shape=[shape(3, CELLS, LANES)] + [shape(9, FACE, LANES)] * 6,
        compiler_params=params,
        name="prepare",
    )(offsets, burgers, lines, counts)
    received = [None] * 6
    for i in (1, 3, 5, 0, 2, 4):
        received[i] = exchanged(sends[i], AXES[i // 2], i % 2)
    masked, *received = lax.optimization_barrier((masked, *received))
    moments = pl.pallas_call(
        moments_kernel,
        in_specs=[vmem, vmem],
        out_shape=shape(256, LANES),
        compiler_params=params,
        name="moments",
    )(masked, lines)
    gathered = lax.all_to_all(
        moments.reshape(256, 1, LANES), AXES, 0, 0, tiled=True
    ).reshape(256, LANES)
    near = pl.pallas_call(
        near_kernel,
        in_specs=[vmem] * 9,
        out_shape=shape(CELLS, 3, LANES),
        scratch_shapes=[
            pltpu.VMEM((SOURCES, DEPTH, LANES), F32),
            pltpu.VMEM((CELLS, DEPTH, LANES), F32),
            pltpu.VMEM((SOURCES, LANES, DEPTH), BF16),
            pltpu.VMEM((CELLS, DEPTH, 2 * LANES), BF16),
            pltpu.VMEM((SOURCES, 16, LANES), BF16),
        ],
        compiler_params=params,
        name="near",
    )(offsets, masked, lines, *received)
    fields, *ends = pl.pallas_call(
        node_kernel,
        in_specs=[vmem] * 4 + [smem] + [vmem] * 3,
        out_shape=[shape(6, 64, LANES), shape(6, 4, LANES), shape(6, 4, LANES)],
        scratch_shapes=[
            pltpu.VMEM((9, CELLS, LANES), F32),
            pltpu.VMEM((288, 256), F32),
            pltpu.VMEM((288, 1024), BF16),
            pltpu.VMEM((256, 1024), BF16),
        ],
        compiler_params=params,
        name="nodes",
    )(gathered, near, masked, lines, stress, connect, node_pos, drag)
    second = exchanged(ends[1], "gx", 1)
    first = exchanged(ends[0], "gx", 0)
    out = pl.pallas_call(
        migrate_kernel,
        in_specs=[vmem] * 3 + [smem],
        out_shape=shape(6, 72, LANES),
        scratch_shapes=[pltpu.VMEM((96, LANES), F32)],
        compiler_params=params,
        name="migrate",
    )(fields, first, second, shifts)
    return out.reshape(6, 1, 1, 1, 72 * LANES)


def solution(mesh):
    cells = P(None, "gx", "gy", "gz", None)
    return jax.shard_map(
        shards,
        mesh=mesh,
        in_specs=(cells, cells, cells, P("gx", "gy", "gz"), cells, cells,
                  P("gx", "gy", "gz", None), P(), P()),
        out_specs=cells,
        check_vma=False,
    )
```

```python
import functools
import jax
import jax.numpy as jnp
from jax import lax
from jax.experimental import pallas as pl
from jax.experimental.pallas import tpu as pltpu
from jax.sharding import PartitionSpec as P

SOFTEN_NEAR = 0.25
SOFTEN_FAR = 4.0
NEAR_SCALE = 0.0625
FAR_SCALE = 0.03125
TIME_STEP = 0.1
AXES = ("gx", "gy", "gz")
F32 = jnp.float32
BF16 = jnp.bfloat16
LANES = 128
DEPTH = 64
CELLS = 64
FACE = 16
SOURCES = CELLS + 6 * FACE
VMEM = 60 << 20


def face_rows(axis):
    return (
        [(0, 48, 16, 1)],
        [(16 * x, 16 * x + 12, 4, 1) for x in range(4)],
        [(0, 3, 16, 4)],
    )[axis]


def split2(value):
    high = value.astype(BF16).astype(F32)
    return high, value - high


def split3(value):
    high = value.astype(BF16).astype(F32)
    rest = value - high
    middle = rest.astype(BF16).astype(F32)
    return high, middle, rest - middle


def prepare_kernel(offsets, burgers, lines, counts, masked, moments, *sends):
    slot = lax.broadcasted_iota(jnp.int32, (8, LANES), 1)
    row = lax.broadcasted_iota(jnp.int32, (8, LANES), 0)
    for group in range(8):
        live = jnp.zeros((8, LANES), jnp.int32)
        for s in range(8):
            cell = 8 * group + s
            live = jnp.where(row == s, counts[cell // 16, (cell // 4) % 4, cell % 4], live)
        for axis in range(3):
            block = burgers[axis, pl.ds(8 * group, 8), :]
            masked[axis, pl.ds(8 * group, 8), :] = jnp.where(slot < live, block, 0.0)
    for axis in range(3):
        even = lax.axis_index(AXES[axis]) % 2 == 0
        to = 0
        for low, high, size, stride in face_rows(axis):
            at_low = pl.ds(low, size, stride=stride) if stride > 1 else pl.ds(low, size)
            at_high = pl.ds(high, size, stride=stride) if stride > 1 else pl.ds(high, size)
            for a in range(3):
                for part, array in enumerate((offsets, masked, lines)):
                    of_low, of_high = array[a, at_low, :], array[a, at_high, :]
                    sends[2 * axis][3 * part + a, pl.ds(to, size), :] = jnp.where(
                        even, of_high, of_low
                    )
                    sends[2 * axis + 1][3 * part + a, pl.ds(to, size), :] = jnp.where(
                        even, of_low, of_high
                    )
            to += size
    rows = []
    for coarse in range(4):
        big_x, big_y = coarse // 2, coarse % 2
        groups = (4 * big_x + big_y, 4 * big_x + 2 + big_y)
        for a in range(3):
            for b in range(3):
                rows.append(
                    sum(
                        masked[a, pl.ds(8 * g, 8), :] * lines[b, pl.ds(8 * g, 8), :]
                        for g in groups
                    )
                )
    stack = jnp.concatenate(rows, axis=0)
    ones = jnp.ones((8, LANES), F32)
    summed = lax.dot_general(
        ones,
        stack,
        (((1,), (1,)), ((), ())),
        precision=lax.Precision.HIGHEST,
        preferred_element_type=F32,
    )
    n = lax.broadcasted_iota(jnp.int32, (288, LANES), 0)
    lane = lax.broadcasted_iota(jnp.int32, (288, LANES), 1)
    target = ((n // 72) * 2 + (n % 4) // 2) * 16 + (n // 8) % 9
    pick = (lane == target).astype(F32)
    packed = jnp.dot(summed, pick, precision=lax.Precision.HIGHEST, preferred_element_type=F32)
    moments[...] = jnp.broadcast_to(packed[0:1], moments.shape)


def source_index(target, lower, upper):
    x, y, z = target >> 4, (target >> 2) & 3, target & 3
    return [
        target,
        jnp.where(x > 0, target - 16, lower[0] + (target & 15)),
        jnp.where(x < 3, target + 16, upper[0] + (target & 15)),
        jnp.where(y > 0, target - 4, lower[1] + x * 4 + z),
        jnp.where(y < 3, target + 4, upper[1] + x * 4 + z),
        jnp.where(z > 0, target - 1, lower[2] + (target >> 2)),
        jnp.where(z < 3, target + 1, upper[2] + (target >> 2)),
    ]


PAIRS = ((0, 0), (0, 1), (1, 0), (0, 2), (2, 0), (1, 1))


def near_kernel(*refs):
    offsets, masked, lines = refs[:3]
    faces = refs[3:9]
    near = refs[9]
    rows_s, rows_t, source, points = refs[10:]
    blocks = []
    for first in range(0, CELLS, 16):
        cell = first + lax.broadcasted_iota(jnp.int32, (16, LANES), 0)
        corner = (cell // 16, (cell // 4) % 4, cell % 4)
        blocks.append(
            (
                first,
                [offsets[a, pl.ds(first, 16), :] + (corner[a].astype(F32) - 2.0) for a in range(3)],
                [masked[a, pl.ds(first, 16), :] for a in range(3)],
                [lines[a, pl.ds(first, 16), :] for a in range(3)],
            )
        )
    cell = lax.broadcasted_iota(jnp.int32, (16, LANES), 0)
    for f, face in enumerate(faces):
        fixed = f // 2
        others = [a for a in range(3) if a != fixed]
        corner = [None] * 3
        upper = lax.axis_index(AXES[fixed]) % 2 == f % 2
        corner[fixed] = jnp.where(upper, 2.0, -3.0).astype(F32)
        corner[others[0]] = (cell // 4).astype(F32) - 2.0
        corner[others[1]] = (cell % 4).astype(F32) - 2.0
        blocks.append(
            (
                CELLS + FACE * f,
                [face[a] + corner[a] for a in range(3)],
                [face[3 + a] for a in range(3)],
                [face[6 + a] for a in range(3)],
            )
        )
    one = jnp.ones((16, LANES), F32)
    rows_s[:, pl.ds(48, DEPTH - 48), :] = jnp.zeros((SOURCES, DEPTH - 48, LANES), F32)
    rows_t[:, pl.ds(48, DEPTH - 48), :] = jnp.zeros((CELLS, DEPTH - 48, LANES), F32)
    for first, place, burger, line in blocks:
        own = first < CELLS
        place_parts = [split3(p) for p in place]
        norm = split3(place[0] * place[0] + place[1] * place[1] + place[2] * place[2])
        outer = [split3(burger[a] * line[b]) for a in range(3) for b in range(3)]
        k = 0
        for s, t in PAIRS:
            for a in range(3):
                rows_s[pl.ds(first, 16), k, :] = place_parts[a][s]
                if own:
                    rows_t[pl.ds(first, 16), k, :] = -2.0 * place_parts[a][t]
                k += 1
        if own:
            shifted = split3(
                place[0] * place[0] + place[1] * place[1] + place[2] * place[2] + SOFTEN_NEAR
            )
        for s in range(3):
            rows_s[pl.ds(first, 16), k, :] = norm[s]
            if own:
                rows_t[pl.ds(first, 16), k, :] = one
            k += 1
        for s in range(3):
            rows_s[pl.ds(first, 16), k, :] = one
            if own:
                rows_t[pl.ds(first, 16), k, :] = shifted[s]
            k += 1
        for s, t in PAIRS[:3]:
            for ab in range(9):
                rows_s[pl.ds(first, 16), k, :] = outer[ab][s]
                if own:
                    rows_t[pl.ds(first, 16), k, :] = outer[ab][t]
                k += 1

    odd = [lax.axis_index(a) & 1 for a in AXES]
    upper = [CELLS + 2 * FACE * a + FACE * odd[a] for a in range(3)]
    lower = [CELLS + 2 * FACE * a + FACE * (1 - odd[a]) for a in range(3)]

    def arrange(c):
        block = rows_s[c]
        source[c] = block.astype(BF16).T
        points[c] = jnp.concatenate(
            [block[0:3], block[6:9], block[12:15], block[21:22], jnp.zeros((6, LANES), F32)],
            axis=0,
        ).astype(BF16)

    together = 8

    def faces_of(i):
        h, x = i & 1, i >> 1
        y_face = jnp.where(h == 0, lower[1], upper[1]) + 4 * x
        z_lower, z_upper = lower[2] + 2 * i, upper[2] + 2 * i
        return [y_face + k for k in range(4)] + [z_lower, z_lower + 1, z_upper, z_upper + 1]

    def first_own(k, carry):
        arrange(k)
        return carry

    def first_lower(k, carry):
        arrange(lower[0] + k)
        return carry

    lax.fori_loop(0, 24, first_own, 0, unroll=8)
    lax.fori_loop(0, FACE, first_lower, 0, unroll=8)
    for c in faces_of(0):
        arrange(c)
    row = lax.broadcasted_iota(jnp.int32, (DEPTH, LANES), 0)

    def step(i, carry):
        following = jnp.minimum(i + 1, CELLS // together - 1)
        ahead = jnp.where(
            following < 6, 8 * following + 16, upper[0] + 8 * (following & 1)
        )
        coming = [ahead + k for k in range(8)] + faces_of(following)
        weights = []
        spots = []
        for u in range(together):
            cell = i * together + u
            sources = source_index(cell, lower, upper)
            block = rows_t[cell]
            stationary = jnp.concatenate(
                [jnp.where(row < 24, block, 0.0), jnp.where(row < 24, 0.0, block)], axis=1
            ).astype(BF16)
            weights.append([])
            for k in range(7):
                pair = jnp.dot(source[sources[k]], stationary, preferred_element_type=F32)
                inverse = lax.rsqrt(pair[:, :LANES])
                weight = pair[:, LANES:] * (inverse * inverse * inverse)
                high = weight.astype(BF16)
                low = (weight - high.astype(F32)).astype(BF16)
                weights[u].append(jnp.concatenate([high, low], axis=1))
            spots.append([points[c] for c in sources])
            for c in coming[2 * u : 2 * u + 2]:
                arrange(c)
        for u in range(together):
            cell = i * together + u
            both = jnp.dot(
                jnp.concatenate(spots[u], axis=1),
                jnp.concatenate(weights[u], axis=0),
                preferred_element_type=F32,
            )
            sums = both[:, :LANES] + both[:, LANES:]
            moved = sums[0:3] + sums[3:6] + sums[6:9]
            base = rows_t[cell, 0:24, :]
            place = -0.5 * (base[0:3] + base[3:6] + base[9:12])
            near[cell] = place * sums[9:10] - moved
        return carry

    lax.fori_loop(0, CELLS // together, step, 0)


def node_kernel(
    gathered, near, masked, lines, stress, connect, node_pos, drag, fields, first, second,
    values, sums,
):
    index_x, index_y, index_z = (lax.axis_index(a) for a in AXES)
    device = lax.broadcasted_iota(jnp.int32, (CELLS, 256), 1)
    cell = lax.broadcasted_iota(jnp.int32, (CELLS, 256), 0)
    gap = [
        (4 * index_x + cell // 16 - 4 * (device // 16)).astype(F32) - 0.5,
        (4 * index_y + (cell // 4) % 4 - 4 * ((device // 4) % 4)).astype(F32) - 0.5,
        (4 * index_z + cell % 4 - 4 * (device % 4)).astype(F32) - 0.5,
    ]
    square = [[gap[a] * gap[a], (gap[a] - 2.0) * (gap[a] - 2.0)] for a in range(3)]
    moments = gathered[...]
    lane = lax.broadcasted_iota(jnp.int32, (CELLS, LANES), 1)
    sigma = jnp.zeros((CELLS, LANES), F32)
    for sub in range(8):
        big_x, big_y, big_z = sub // 4, (sub // 2) % 2, sub % 2
        weight = lax.rsqrt(square[0][big_x] + square[1][big_y] + square[2][big_z] + SOFTEN_FAR)
        part = jnp.dot(
            weight, moments, precision=lax.Precision.HIGHEST, preferred_element_type=F32
        )
        sigma = jnp.where(lane // 16 == sub, part, sigma)
    for shift in (64, 32, 16):
        sigma = sigma + pltpu.roll(sigma, shift, 1)
    pull = [
        [FAR_SCALE * sigma[:, 3 * a + b : 3 * a + b + 1] + stress[a, b] for b in range(3)]
        for a in range(3)
    ]
    burger = [masked[a] for a in range(3)]
    line = [lines[a] for a in range(3)]
    pulled = [
        pull[a][0] * burger[0] + pull[a][1] * burger[1] + pull[a][2] * burger[2] for a in range(3)
    ]
    for a in range(3):
        b, c = (a + 1) % 3, (a + 2) % 3
        force = NEAR_SCALE * near[:, a, :] + (pulled[b] * line[c] - pulled[c] * line[b])
        high, rest = split2(0.5 * force)
        values[a] = high
        values[3 + a] = rest
    sums[...] = jnp.zeros(sums.shape, F32)
    rows_high = lax.broadcasted_iota(jnp.int32, (32, LANES), 0)
    rows_low = lax.broadcasted_iota(jnp.int32, (256, LANES), 0)
    step_cells = 16

    def scatter(i, carry):
        left, right = [], []
        for u in range(step_cells):
            at = i * step_cells + u
            for end in range(2):
                node = connect[end, pl.ds(at, 1), :]
                chosen = rows_high == (node >> 8)
                left.append(
                    jnp.concatenate(
                        [jnp.where(chosen, values[q, pl.ds(at, 1), :], 0.0) for q in range(6)],
                        axis=0,
                    ).astype(BF16)
                )
                right.append((rows_low == (node & 255)).astype(F32).astype(BF16))
        sums[...] += lax.dot_general(
            jnp.concatenate(left, axis=1),
            jnp.concatenate(right, axis=1),
            (((1,), (1,)), ((), ())),
            preferred_element_type=F32,
        )
        return carry

    lax.fori_loop(0, CELLS // step_cells, scatter, 0, unroll=1)
    for a in range(3):
        force = sums[pl.ds(32 * a, 32), :] + sums[pl.ds(96 + 32 * a, 32), :]
        fields[3 + a, pl.ds(0, 32, stride=2), :] = force[:, :LANES]
        fields[3 + a, pl.ds(1, 32, stride=2), :] = force[:, LANES:]
    for a in range(3):
        velocity = fields[3 + a] / drag[...]
        fields[3 + a] = velocity
        fields[a] = node_pos[a] + TIME_STEP * velocity
    even = index_x % 2 == 0
    for a in range(6):
        tail = fields[a, pl.ds(60, 4), :]
        head = fields[a, pl.ds(0, 4), :]
        first[a] = jnp.where(even, tail, head)
        second[a] = jnp.where(even, head, tail)


def migrate_kernel(fields, first, second, shifts, out, joined):
    index_x, index_y, index_z = (lax.axis_index(a) for a in AXES)
    last = lax.axis_size("gx") - 1
    even = index_x % 2 == 0
    up_own = shifts[0, index_y, index_z, index_x]
    down_own = shifts[1, index_y, index_z, index_x]
    up_prev = jnp.where(
        index_x > 0, shifts[0, index_y, index_z, jnp.maximum(index_x - 1, 0)], 0
    )
    down_next = jnp.where(
        index_x < last, shifts[1, index_y, index_z, jnp.minimum(index_x + 1, last)], 0
    )
    kept = 8192 - up_own - down_own
    row = lax.broadcasted_iota(jnp.int32, (72, LANES), 0)
    lane = lax.broadcasted_iota(jnp.int32, (72, LANES), 1)
    position = row * LANES + lane
    pieces = (
        (512 - up_prev, position < up_prev),
        (512 + down_own - up_prev, position < up_prev + kept),
        (8704 - up_prev - kept, position < up_prev + kept + down_next),
    )
    for a in range(6):
        joined[pl.ds(0, 4), :] = jnp.where(even, second[a], first[a])
        joined[pl.ds(4, 64), :] = fields[a]
        joined[pl.ds(68, 4), :] = jnp.where(even, first[a], second[a])
        result = jnp.zeros((72, LANES), F32)
        for delta, within in reversed(pieces):
            rows, lanes = delta >> 7, delta & 127
            here = pltpu.roll(joined[pl.ds(rows, 72), :], (LANES - lanes) & 127, 1)
            after = pltpu.roll(joined[pl.ds(rows + 1, 72), :], (LANES - lanes) & 127, 1)
            moved = jnp.where(lane < LANES - lanes, here, after)
            result = jnp.where(within, moved, result)
        out[a] = result


def exchanged(array, axis, first):
    pairs = [(i, i + 1) for i in range(first, lax.axis_size(axis) - 1, 2)]
    return lax.ppermute(array, axis, pairs + [(b, a) for a, b in pairs])


def shape(*dims, dtype=F32):
    return pltpu.VMEM(dims, dtype)


def on_chip(array):
    return pltpu.with_memory_space_constraint(array, pltpu.VMEM)


def shards(offsets, burgers, lines, counts, connect, node_pos, drag, stress, shifts):
    offsets = offsets.reshape(3, CELLS, LANES)
    burgers = burgers.reshape(3, CELLS, LANES)
    lines = lines.reshape(3, CELLS, LANES)
    connect = connect.reshape(2, CELLS, LANES)
    node_pos = node_pos.reshape(3, 64, LANES)
    drag = drag.reshape(64, LANES)
    shifts = shifts.transpose(0, 2, 3, 1)
    vmem = pl.BlockSpec(memory_space=pltpu.VMEM)
    smem = pl.BlockSpec(memory_space=pltpu.SMEM)
    params = pltpu.CompilerParams(vmem_limit_bytes=VMEM)
    masked, moments, *sends = pl.pallas_call(
        prepare_kernel,
        in_specs=[vmem, vmem, vmem, smem],
        out_shape=[shape(3, CELLS, LANES), shape(256, LANES)] + [shape(9, FACE, LANES)] * 6,
        compiler_params=params,
        name="prepare",
    )(offsets, burgers, lines, counts)
    received = [None] * 6
    for i in (1, 3, 5, 0, 2, 4):
        received[i] = exchanged(sends[i], AXES[i // 2], i % 2)
    moments, *received = lax.optimization_barrier((moments, *received))
    gathered = lax.all_to_all(
        moments.reshape(256, 1, LANES), AXES, 0, 0, tiled=True
    ).reshape(256, LANES)
    near = pl.pallas_call(
        near_kernel,
        in_specs=[vmem] * 9,
        out_shape=shape(CELLS, 3, LANES),
        scratch_shapes=[
            pltpu.VMEM((SOURCES, DEPTH, LANES), F32),
            pltpu.VMEM((CELLS, DEPTH, LANES), F32),
            pltpu.VMEM((SOURCES, LANES, DEPTH), BF16),
            pltpu.VMEM((SOURCES, 16, LANES), BF16),
        ],
        compiler_params=params,
        name="near",
    )(offsets, on_chip(masked), lines, *[on_chip(face) for face in received])
    fields, *ends = pl.pallas_call(
        node_kernel,
        in_specs=[vmem] * 4 + [smem] + [vmem] * 3,
        out_shape=[shape(6, 64, LANES), shape(6, 4, LANES), shape(6, 4, LANES)],
        scratch_shapes=[
            pltpu.VMEM((6, CELLS, LANES), F32),
            pltpu.VMEM((192, 256), F32),
        ],
        compiler_params=params,
        name="nodes",
    )(on_chip(gathered), on_chip(near), on_chip(masked), lines, stress, connect, node_pos, drag)
    second = exchanged(ends[1], "gx", 1)
    first = exchanged(ends[0], "gx", 0)
    out = pl.pallas_call(
        migrate_kernel,
        in_specs=[vmem] * 3 + [smem],
        out_shape=jax.ShapeDtypeStruct((6, 72, LANES), F32),
        scratch_shapes=[pltpu.VMEM((96, LANES), F32)],
        compiler_params=params,
        name="migrate",
    )(on_chip(fields), on_chip(first), on_chip(second), shifts)
    return out.reshape(6, 1, 1, 1, 72 * LANES)


def solution(mesh):
    cells = P(None, "gx", "gy", "gz", None)
    return jax.shard_map(
        shards,
        mesh=mesh,
        in_specs=(cells, cells, cells, P("gx", "gy", "gz"), cells, cells,
                  P("gx", "gy", "gz", None), P(), P()),
        out_specs=cells,
        check_vma=False,
    )
```

```python
import functools
import jax
import jax.numpy as jnp
from jax import lax
from jax.experimental import pallas as pl
from jax.experimental.pallas import tpu as pltpu
from jax.sharding import PartitionSpec as P

SOFTEN_NEAR = 0.25
SOFTEN_FAR = 4.0
NEAR_SCALE = 0.0625
FAR_SCALE = 0.03125
TIME_STEP = 0.1
AXES = ("gx", "gy", "gz")
F32 = jnp.float32
BF16 = jnp.bfloat16
LANES = 128
DEPTH = 64
STEP_CELLS = 16
CELLS = 64
FACE = 16
SOURCES = CELLS + 6 * FACE
VMEM = 60 << 20


def face_rows(axis):
    return (
        [(0, 48, 16, 1)],
        [(16 * x, 16 * x + 12, 4, 1) for x in range(4)],
        [(0, 3, 16, 4)],
    )[axis]


def split2(value):
    high = value.astype(BF16).astype(F32)
    return high, value - high


def split3(value):
    high = value.astype(BF16).astype(F32)
    rest = value - high
    middle = rest.astype(BF16).astype(F32)
    return high, middle, rest - middle


def prepare_kernel(offsets, burgers, lines, counts, masked, moments, *sends):
    slot = lax.broadcasted_iota(jnp.int32, (8, LANES), 1)
    row = lax.broadcasted_iota(jnp.int32, (8, LANES), 0)
    for group in range(8):
        live = jnp.zeros((8, LANES), jnp.int32)
        for s in range(8):
            cell = 8 * group + s
            live = jnp.where(row == s, counts[cell // 16, (cell // 4) % 4, cell % 4], live)
        for axis in range(3):
            block = burgers[axis, pl.ds(8 * group, 8), :]
            masked[axis, pl.ds(8 * group, 8), :] = jnp.where(slot < live, block, 0.0)
    for axis in range(3):
        even = lax.axis_index(AXES[axis]) % 2 == 0
        to = 0
        for low, high, size, stride in face_rows(axis):
            at_low = pl.ds(low, size, stride=stride) if stride > 1 else pl.ds(low, size)
            at_high = pl.ds(high, size, stride=stride) if stride > 1 else pl.ds(high, size)
            for a in range(3):
                for part, array in enumerate((offsets, masked, lines)):
                    of_low, of_high = array[a, at_low, :], array[a, at_high, :]
                    sends[2 * axis][3 * part + a, pl.ds(to, size), :] = jnp.where(
                        even, of_high, of_low
                    )
                    sends[2 * axis + 1][3 * part + a, pl.ds(to, size), :] = jnp.where(
                        even, of_low, of_high
                    )
            to += size
    rows = []
    for coarse in range(4):
        big_x, big_y = coarse // 2, coarse % 2
        groups = (4 * big_x + big_y, 4 * big_x + 2 + big_y)
        for a in range(3):
            for b in range(3):
                rows.append(
                    sum(
                        masked[a, pl.ds(8 * g, 8), :] * lines[b, pl.ds(8 * g, 8), :]
                        for g in groups
                    )
                )
    stack = jnp.concatenate(rows, axis=0)
    ones = jnp.ones((8, LANES), F32)
    summed = lax.dot_general(
        ones,
        stack,
        (((1,), (1,)), ((), ())),
        precision=lax.Precision.HIGHEST,
        preferred_element_type=F32,
    )
    n = lax.broadcasted_iota(jnp.int32, (288, LANES), 0)
    lane = lax.broadcasted_iota(jnp.int32, (288, LANES), 1)
    target = ((n // 72) * 2 + (n % 4) // 2) * 16 + (n // 8) % 9
    pick = (lane == target).astype(F32)
    packed = jnp.dot(summed, pick, precision=lax.Precision.HIGHEST, preferred_element_type=F32)
    moments[...] = jnp.broadcast_to(packed[0:1], moments.shape)


def source_index(target, lower, upper):
    x, y, z = target >> 4, (target >> 2) & 3, target & 3
    return [
        target,
        jnp.where(x > 0, target - 16, lower[0] + (target & 15)),
        jnp.where(x < 3, target + 16, upper[0] + (target & 15)),
        jnp.where(y > 0, target - 4, lower[1] + x * 4 + z),
        jnp.where(y < 3, target + 4, upper[1] + x * 4 + z),
        jnp.where(z > 0, target - 1, lower[2] + (target >> 2)),
        jnp.where(z < 3, target + 1, upper[2] + (target >> 2)),
    ]


PAIRS = ((0, 0), (0, 1), (1, 0), (0, 2), (2, 0), (1, 1))


def near_kernel(*refs):
    offsets, masked, lines = refs[:3]
    faces = refs[3:9]
    near = refs[9]
    rows_s, rows_t, source, points = refs[10:]
    blocks = []
    for first in range(0, CELLS, 16):
        cell = first + lax.broadcasted_iota(jnp.int32, (16, LANES), 0)
        corner = (cell // 16, (cell // 4) % 4, cell % 4)
        blocks.append(
            (
                first,
                [offsets[a, pl.ds(first, 16), :] + (corner[a].astype(F32) - 2.0) for a in range(3)],
                [masked[a, pl.ds(first, 16), :] for a in range(3)],
                [lines[a, pl.ds(first, 16), :] for a in range(3)],
            )
        )
    cell = lax.broadcasted_iota(jnp.int32, (16, LANES), 0)
    for f, face in enumerate(faces):
        fixed = f // 2
        others = [a for a in range(3) if a != fixed]
        corner = [None] * 3
        upper = lax.axis_index(AXES[fixed]) % 2 == f % 2
        corner[fixed] = jnp.where(upper, 2.0, -3.0).astype(F32)
        corner[others[0]] = (cell // 4).astype(F32) - 2.0
        corner[others[1]] = (cell % 4).astype(F32) - 2.0
        blocks.append(
            (
                CELLS + FACE * f,
                [face[a] + corner[a] for a in range(3)],
                [face[3 + a] for a in range(3)],
                [face[6 + a] for a in range(3)],
            )
        )
    one = jnp.ones((16, LANES), F32)
    rows_s[:, pl.ds(48, DEPTH - 48), :] = jnp.zeros((SOURCES, DEPTH - 48, LANES), F32)
    rows_t[:, pl.ds(48, DEPTH - 48), :] = jnp.zeros((CELLS, DEPTH - 48, LANES), F32)
    for first, place, burger, line in blocks:
        own = first < CELLS
        place_parts = [split3(p) for p in place]
        norm = split3(place[0] * place[0] + place[1] * place[1] + place[2] * place[2])
        outer = [split3(burger[a] * line[b]) for a in range(3) for b in range(3)]
        k = 0
        for s, t in PAIRS:
            for a in range(3):
                rows_s[pl.ds(first, 16), k, :] = place_parts[a][s]
                if own:
                    rows_t[pl.ds(first, 16), k, :] = -2.0 * place_parts[a][t]
                k += 1
        if own:
            shifted = split3(
                place[0] * place[0] + place[1] * place[1] + place[2] * place[2] + SOFTEN_NEAR
            )
        for s in range(3):
            rows_s[pl.ds(first, 16), k, :] = norm[s]
            if own:
                rows_t[pl.ds(first, 16), k, :] = one
            k += 1
        for s in range(3):
            rows_s[pl.ds(first, 16), k, :] = one
            if own:
                rows_t[pl.ds(first, 16), k, :] = shifted[s]
            k += 1
        for s, t in PAIRS[:3]:
            for ab in range(9):
                rows_s[pl.ds(first, 16), k, :] = outer[ab][s]
                if own:
                    rows_t[pl.ds(first, 16), k, :] = outer[ab][t]
                k += 1

    odd = [lax.axis_index(a) & 1 for a in AXES]
    upper = [CELLS + 2 * FACE * a + FACE * odd[a] for a in range(3)]
    lower = [CELLS + 2 * FACE * a + FACE * (1 - odd[a]) for a in range(3)]

    def arrange(c):
        block = rows_s[c]
        source[c] = block.astype(BF16).T
        points[c] = jnp.concatenate(
            [block[0:3], block[6:9], block[12:15], block[21:22], jnp.zeros((6, LANES), F32)],
            axis=0,
        ).astype(BF16)

    together = 8

    def faces_of(i):
        h, x = i & 1, i >> 1
        y_face = jnp.where(h == 0, lower[1], upper[1]) + 4 * x
        z_lower, z_upper = lower[2] + 2 * i, upper[2] + 2 * i
        return [y_face + k for k in range(4)] + [z_lower, z_lower + 1, z_upper, z_upper + 1]

    def first_own(k, carry):
        arrange(k)
        return carry

    def first_lower(k, carry):
        arrange(lower[0] + k)
        return carry

    lax.fori_loop(0, 24, first_own, 0, unroll=8)
    lax.fori_loop(0, FACE, first_lower, 0, unroll=8)
    for c in faces_of(0):
        arrange(c)
    row = lax.broadcasted_iota(jnp.int32, (DEPTH, LANES), 0)

    def step(i, carry):
        following = jnp.minimum(i + 1, CELLS // together - 1)
        ahead = jnp.where(
            following < 6, 8 * following + 16, upper[0] + 8 * (following & 1)
        )
        coming = [ahead + k for k in range(8)] + faces_of(following)
        weights = []
        spots = []
        for u in range(together):
            cell = i * together + u
            sources = source_index(cell, lower, upper)
            block = rows_t[cell]
            stationary = jnp.concatenate(
                [jnp.where(row < 24, block, 0.0), jnp.where(row < 24, 0.0, block)], axis=1
            ).astype(BF16)
            weights.append([])
            for k in range(7):
                pair = jnp.dot(source[sources[k]], stationary, preferred_element_type=F32)
                inverse = lax.rsqrt(pair[:, :LANES])
                weight = pair[:, LANES:] * (inverse * inverse * inverse)
                high = weight.astype(BF16)
                low = (weight - high.astype(F32)).astype(BF16)
                weights[u].append(jnp.concatenate([high, low], axis=1))
            spots.append([points[c] for c in sources])
            for c in coming[2 * u : 2 * u + 2]:
                arrange(c)
        for u in range(together):
            cell = i * together + u
            both = jnp.dot(
                jnp.concatenate(spots[u], axis=1),
                jnp.concatenate(weights[u], axis=0),
                preferred_element_type=F32,
            )
            sums = both[:, :LANES] + both[:, LANES:]
            moved = sums[0:3] + sums[3:6] + sums[6:9]
            base = rows_t[cell, 0:24, :]
            place = -0.5 * (base[0:3] + base[3:6] + base[9:12])
            near[cell] = place * sums[9:10] - moved
        return carry

    lax.fori_loop(0, CELLS // together, step, 0)


def force_kernel(
    gathered, near, masked, lines, stress, connect, node_pos, drag, values, first, second
):
    index_x, index_y, index_z = (lax.axis_index(a) for a in AXES)
    device = lax.broadcasted_iota(jnp.int32, (CELLS, 256), 1)
    cell = lax.broadcasted_iota(jnp.int32, (CELLS, 256), 0)
    gap = [
        (4 * index_x + cell // 16 - 4 * (device // 16)).astype(F32) - 0.5,
        (4 * index_y + (cell // 4) % 4 - 4 * ((device // 4) % 4)).astype(F32) - 0.5,
        (4 * index_z + cell % 4 - 4 * (device % 4)).astype(F32) - 0.5,
    ]
    square = [[gap[a] * gap[a], (gap[a] - 2.0) * (gap[a] - 2.0)] for a in range(3)]
    moments = gathered[...]
    lane = lax.broadcasted_iota(jnp.int32, (CELLS, LANES), 1)
    sigma = jnp.zeros((CELLS, LANES), F32)
    for sub in range(8):
        big_x, big_y, big_z = sub // 4, (sub // 2) % 2, sub % 2
        weight = lax.rsqrt(square[0][big_x] + square[1][big_y] + square[2][big_z] + SOFTEN_FAR)
        part = jnp.dot(
            weight, moments, precision=lax.Precision.HIGHEST, preferred_element_type=F32
        )
        sigma = jnp.where(lane // 16 == sub, part, sigma)
    for shift in (64, 32, 16):
        sigma = sigma + pltpu.roll(sigma, shift, 1)
    pull = [
        [FAR_SCALE * sigma[:, 3 * a + b : 3 * a + b + 1] + stress[a, b] for b in range(3)]
        for a in range(3)
    ]
    burger = [masked[a] for a in range(3)]
    line = [lines[a] for a in range(3)]
    pulled = [
        pull[a][0] * burger[0] + pull[a][1] * burger[1] + pull[a][2] * burger[2] for a in range(3)
    ]
    for a in range(3):
        b, c = (a + 1) % 3, (a + 2) % 3
        force = NEAR_SCALE * near[:, a, :] + (pulled[b] * line[c] - pulled[c] * line[b])
        high, rest = split2(0.5 * force)
        values[a] = high
        values[3 + a] = rest
    rows_high = lax.broadcasted_iota(jnp.int32, (8, LANES), 0)
    rows_low = lax.broadcasted_iota(jnp.int32, (LANES, LANES), 0)

    def scatter(i, total):
        left, right = [], []
        for u in range(STEP_CELLS):
            at = i * STEP_CELLS + u
            for end in range(2):
                node = connect[end, pl.ds(at, 1), :]
                high = node >> 7
                high = jnp.where(high < 4, high, high - 56)
                high = jnp.where((node < 512) | (node >= 7680), high, -1)
                chosen = rows_high == high
                left.append(
                    jnp.concatenate(
                        [jnp.where(chosen, values[q, pl.ds(at, 1), :], 0.0) for q in range(6)],
                        axis=0,
                    ).astype(BF16)
                )
                right.append((rows_low == (node & 127)).astype(F32).astype(BF16))
        return total + lax.dot_general(
            jnp.concatenate(left, axis=1),
            jnp.concatenate(right, axis=1),
            (((1,), (1,)), ((), ())),
            preferred_element_type=F32,
        )

    total = lax.fori_loop(0, CELLS // STEP_CELLS, scatter, jnp.zeros((48, LANES), F32))
    even = index_x % 2 == 0
    for a in range(3):
        force = total[8 * a : 8 * a + 8] + total[24 + 8 * a : 32 + 8 * a]
        slow = jnp.concatenate([drag[pl.ds(0, 4), :], drag[pl.ds(60, 4), :]], axis=0)
        place = jnp.concatenate([node_pos[a, pl.ds(0, 4), :], node_pos[a, pl.ds(60, 4), :]], axis=0)
        velocity = force / slow
        for row, field in ((a, place + TIME_STEP * velocity), (3 + a, velocity)):
            head, tail = field[0:4], field[4:8]
            first[row] = jnp.where(even, tail, head)
            second[row] = jnp.where(even, head, tail)


def node_kernel(values, connect, node_pos, drag, fields, sums):
    sums[...] = jnp.zeros(sums.shape, F32)
    rows_high = lax.broadcasted_iota(jnp.int32, (32, LANES), 0)
    rows_low = lax.broadcasted_iota(jnp.int32, (256, LANES), 0)

    def scatter(i, carry):
        left, right = [], []
        for u in range(STEP_CELLS):
            at = i * STEP_CELLS + u
            for end in range(2):
                node = connect[end, pl.ds(at, 1), :]
                chosen = rows_high == (node >> 8)
                left.append(
                    jnp.concatenate(
                        [jnp.where(chosen, values[q, pl.ds(at, 1), :], 0.0) for q in range(6)],
                        axis=0,
                    ).astype(BF16)
                )
                right.append((rows_low == (node & 255)).astype(F32).astype(BF16))
        sums[...] += lax.dot_general(
            jnp.concatenate(left, axis=1),
            jnp.concatenate(right, axis=1),
            (((1,), (1,)), ((), ())),
            preferred_element_type=F32,
        )
        return carry

    lax.fori_loop(0, CELLS // STEP_CELLS, scatter, 0, unroll=1)
    for a in range(3):
        force = sums[pl.ds(32 * a, 32), :] + sums[pl.ds(96 + 32 * a, 32), :]
        fields[3 + a, pl.ds(0, 32, stride=2), :] = force[:, :LANES]
        fields[3 + a, pl.ds(1, 32, stride=2), :] = force[:, LANES:]
    for a in range(3):
        velocity = fields[3 + a] / drag[...]
        fields[3 + a] = velocity
        fields[a] = node_pos[a] + TIME_STEP * velocity


def migrate_kernel(fields, first, second, shifts, out, joined):
    index_x, index_y, index_z = (lax.axis_index(a) for a in AXES)
    last = lax.axis_size("gx") - 1
    even = index_x % 2 == 0
    up_own = shifts[0, index_y, index_z, index_x]
    down_own = shifts[1, index_y, index_z, index_x]
    up_prev = jnp.where(
        index_x > 0, shifts[0, index_y, index_z, jnp.maximum(index_x - 1, 0)], 0
    )
    down_next = jnp.where(
        index_x < last, shifts[1, index_y, index_z, jnp.minimum(index_x + 1, last)], 0
    )
    kept = 8192 - up_own - down_own
    row = lax.broadcasted_iota(jnp.int32, (72, LANES), 0)
    lane = lax.broadcasted_iota(jnp.int32, (72, LANES), 1)
    position = row * LANES + lane
    pieces = (
        (512 - up_prev, position < up_prev),
        (512 + down_own - up_prev, position < up_prev + kept),
        (8704 - up_prev - kept, position < up_prev + kept + down_next),
    )
    for a in range(6):
        joined[pl.ds(0, 4), :] = jnp.where(even, second[a], first[a])
        joined[pl.ds(4, 64), :] = fields[a]
        joined[pl.ds(68, 4), :] = jnp.where(even, first[a], second[a])
        result = jnp.zeros((72, LANES), F32)
        for delta, within in reversed(pieces):
            rows, lanes = delta >> 7, delta & 127
            here = pltpu.roll(joined[pl.ds(rows, 72), :], (LANES - lanes) & 127, 1)
            after = pltpu.roll(joined[pl.ds(rows + 1, 72), :], (LANES - lanes) & 127, 1)
            moved = jnp.where(lane < LANES - lanes, here, after)
            result = jnp.where(within, moved, result)
        out[a] = result


def exchanged(array, axis, first):
    pairs = [(i, i + 1) for i in range(first, lax.axis_size(axis) - 1, 2)]
    return lax.ppermute(array, axis, pairs + [(b, a) for a, b in pairs])


def shape(*dims, dtype=F32):
    return pltpu.VMEM(dims, dtype)


def on_chip(array):
    return pltpu.with_memory_space_constraint(array, pltpu.VMEM)


def shards(offsets, burgers, lines, counts, connect, node_pos, drag, stress, shifts):
    offsets = offsets.reshape(3, CELLS, LANES)
    burgers = burgers.reshape(3, CELLS, LANES)
    lines = lines.reshape(3, CELLS, LANES)
    connect = connect.reshape(2, CELLS, LANES)
    node_pos = node_pos.reshape(3, 64, LANES)
    drag = drag.reshape(64, LANES)
    shifts = shifts.transpose(0, 2, 3, 1)
    vmem = pl.BlockSpec(memory_space=pltpu.VMEM)
    smem = pl.BlockSpec(memory_space=pltpu.SMEM)
    params = pltpu.CompilerParams(vmem_limit_bytes=VMEM)
    masked, moments, *sends = pl.pallas_call(
        prepare_kernel,
        in_specs=[vmem, vmem, vmem, smem],
        out_shape=[shape(3, CELLS, LANES), shape(256, LANES)] + [shape(9, FACE, LANES)] * 6,
        compiler_params=params,
        name="prepare",
    )(offsets, burgers, lines, counts)
    received = [None] * 6
    for i in (1, 3, 5, 0, 2, 4):
        received[i] = exchanged(sends[i], AXES[i // 2], i % 2)
    moments, *received = lax.optimization_barrier((moments, *received))
    gathered = lax.all_to_all(
        moments.reshape(256, 1, LANES), AXES, 0, 0, tiled=True
    ).reshape(256, LANES)
    near = pl.pallas_call(
        near_kernel,
        in_specs=[vmem] * 9,
        out_shape=shape(CELLS, 3, LANES),
        scratch_shapes=[
            pltpu.VMEM((SOURCES, DEPTH, LANES), F32),
            pltpu.VMEM((CELLS, DEPTH, LANES), F32),
            pltpu.VMEM((SOURCES, LANES, DEPTH), BF16),
            pltpu.VMEM((SOURCES, 16, LANES), BF16),
        ],
        compiler_params=params,
        name="near",
    )(offsets, on_chip(masked), lines, *[on_chip(face) for face in received])
    values, *ends = pl.pallas_call(
        force_kernel,
        in_specs=[vmem] * 4 + [smem] + [vmem] * 3,
        out_shape=[shape(6, CELLS, LANES), shape(6, 4, LANES), shape(6, 4, LANES)],
        compiler_params=params,
        name="forces",
    )(on_chip(gathered), on_chip(near), on_chip(masked), lines, stress, connect, node_pos, drag)
    second = exchanged(ends[1], "gx", 1)
    first = exchanged(ends[0], "gx", 0)
    fields = pl.pallas_call(
        node_kernel,
        in_specs=[vmem] * 4,
        out_shape=shape(6, 64, LANES),
        scratch_shapes=[pltpu.VMEM((192, 256), F32)],
        compiler_params=params,
        name="nodes",
    )(on_chip(values), connect, node_pos, drag)
    out = pl.pallas_call(
        migrate_kernel,
        in_specs=[vmem] * 3 + [smem],
        out_shape=jax.ShapeDtypeStruct((6, 72, LANES), F32),
        scratch_shapes=[pltpu.VMEM((96, LANES), F32)],
        compiler_params=params,
        name="migrate",
    )(on_chip(fields), on_chip(first), on_chip(second), shifts)
    return out.reshape(6, 1, 1, 1, 72 * LANES)


def solution(mesh):
    cells = P(None, "gx", "gy", "gz", None)
    return jax.shard_map(
        shards,
        mesh=mesh,
        in_specs=(cells, cells, cells, P("gx", "gy", "gz"), cells, cells,
                  P("gx", "gy", "gz", None), P(), P()),
        out_specs=cells,
        check_vma=False,
    )
```

```python
import functools
import jax
import jax.numpy as jnp
from jax import lax
from jax.experimental import pallas as pl
from jax.experimental.pallas import tpu as pltpu
from jax.sharding import PartitionSpec as P

SOFTEN_NEAR = 0.25
SOFTEN_FAR = 4.0
NEAR_SCALE = 0.0625
FAR_SCALE = 0.03125
TIME_STEP = 0.1
AXES = ("gx", "gy", "gz")
F32 = jnp.float32
BF16 = jnp.bfloat16
LANES = 128
DEPTH = 64
STEP_CELLS = 16
ORDER = (1, 3, 5, 2, 4, 0)
CELLS = 64
FACE = 16
SOURCES = CELLS + 6 * FACE
VMEM = 60 << 20


def face_rows(axis):
    return (
        [(0, 48, 16, 1)],
        [(16 * x, 16 * x + 12, 4, 1) for x in range(4)],
        [(0, 3, 16, 4)],
    )[axis]


def split2(value):
    high = value.astype(BF16).astype(F32)
    return high, value - high


def split3(value):
    high = value.astype(BF16).astype(F32)
    rest = value - high
    middle = rest.astype(BF16).astype(F32)
    return high, middle, rest - middle


def prepare_kernel(offsets, burgers, lines, counts, masked, moments, *sends):
    slot = lax.broadcasted_iota(jnp.int32, (8, LANES), 1)
    row = lax.broadcasted_iota(jnp.int32, (8, LANES), 0)
    for group in range(8):
        live = jnp.zeros((8, LANES), jnp.int32)
        for s in range(8):
            cell = 8 * group + s
            live = jnp.where(row == s, counts[cell // 16, (cell // 4) % 4, cell % 4], live)
        for axis in range(3):
            block = burgers[axis, pl.ds(8 * group, 8), :]
            masked[axis, pl.ds(8 * group, 8), :] = jnp.where(slot < live, block, 0.0)
    sends = [sends[ORDER.index(i)] for i in range(6)]
    for axis in range(3):
        even = lax.axis_index(AXES[axis]) % 2 == 0
        to = 0
        for low, high, size, stride in face_rows(axis):
            at_low = pl.ds(low, size, stride=stride) if stride > 1 else pl.ds(low, size)
            at_high = pl.ds(high, size, stride=stride) if stride > 1 else pl.ds(high, size)
            for a in range(3):
                for part, array in enumerate((offsets, masked, lines)):
                    of_low, of_high = array[a, at_low, :], array[a, at_high, :]
                    sends[2 * axis][3 * part + a, pl.ds(to, size), :] = jnp.where(
                        even, of_high, of_low
                    )
                    sends[2 * axis + 1][3 * part + a, pl.ds(to, size), :] = jnp.where(
                        even, of_low, of_high
                    )
            to += size
    rows = []
    for coarse in range(4):
        big_x, big_y = coarse // 2, coarse % 2
        groups = (4 * big_x + big_y, 4 * big_x + 2 + big_y)
        for a in range(3):
            for b in range(3):
                rows.append(
                    sum(
                        masked[a, pl.ds(8 * g, 8), :] * lines[b, pl.ds(8 * g, 8), :]
                        for g in groups
                    )
                )
    stack = jnp.concatenate(rows, axis=0)
    ones = jnp.ones((8, LANES), F32)
    summed = lax.dot_general(
        ones,
        stack,
        (((1,), (1,)), ((), ())),
        precision=lax.Precision.HIGHEST,
        preferred_element_type=F32,
    )
    n = lax.broadcasted_iota(jnp.int32, (288, LANES), 0)
    lane = lax.broadcasted_iota(jnp.int32, (288, LANES), 1)
    target = ((n // 72) * 2 + (n % 4) // 2) * 16 + (n // 8) % 9
    pick = (lane == target).astype(F32)
    packed = jnp.dot(summed, pick, precision=lax.Precision.HIGHEST, preferred_element_type=F32)
    moments[...] = jnp.broadcast_to(packed[0:1], moments.shape)


def source_index(target, lower, upper):
    x, y, z = target >> 4, (target >> 2) & 3, target & 3
    return [
        target,
        jnp.where(x > 0, target - 16, lower[0] + (target & 15)),
        jnp.where(x < 3, target + 16, upper[0] + (target & 15)),
        jnp.where(y > 0, target - 4, lower[1] + x * 4 + z),
        jnp.where(y < 3, target + 4, upper[1] + x * 4 + z),
        jnp.where(z > 0, target - 1, lower[2] + (target >> 2)),
        jnp.where(z < 3, target + 1, upper[2] + (target >> 2)),
    ]


PAIRS = ((0, 0), (0, 1), (1, 0), (0, 2), (2, 0), (1, 1))


def near_kernel(*refs):
    offsets, masked, lines = refs[:3]
    faces = refs[3:9]
    near = refs[9]
    rows_s, rows_t, source, points = refs[10:]
    blocks = []
    for first in range(0, CELLS, 16):
        cell = first + lax.broadcasted_iota(jnp.int32, (16, LANES), 0)
        corner = (cell // 16, (cell // 4) % 4, cell % 4)
        blocks.append(
            (
                first,
                [offsets[a, pl.ds(first, 16), :] + (corner[a].astype(F32) - 2.0) for a in range(3)],
                [masked[a, pl.ds(first, 16), :] for a in range(3)],
                [lines[a, pl.ds(first, 16), :] for a in range(3)],
            )
        )
    cell = lax.broadcasted_iota(jnp.int32, (16, LANES), 0)
    for f, face in enumerate(faces):
        fixed = f // 2
        others = [a for a in range(3) if a != fixed]
        corner = [None] * 3
        upper = lax.axis_index(AXES[fixed]) % 2 == f % 2
        corner[fixed] = jnp.where(upper, 2.0, -3.0).astype(F32)
        corner[others[0]] = (cell // 4).astype(F32) - 2.0
        corner[others[1]] = (cell % 4).astype(F32) - 2.0
        blocks.append(
            (
                CELLS + FACE * f,
                [face[a] + corner[a] for a in range(3)],
                [face[3 + a] for a in range(3)],
                [face[6 + a] for a in range(3)],
            )
        )
    one = jnp.ones((16, LANES), F32)
    rows_s[:, pl.ds(48, DEPTH - 48), :] = jnp.zeros((SOURCES, DEPTH - 48, LANES), F32)
    rows_t[:, pl.ds(48, DEPTH - 48), :] = jnp.zeros((CELLS, DEPTH - 48, LANES), F32)
    for first, place, burger, line in blocks:
        own = first < CELLS
        place_parts = [split3(p) for p in place]
        norm = split3(place[0] * place[0] + place[1] * place[1] + place[2] * place[2])
        outer = [split3(burger[a] * line[b]) for a in range(3) for b in range(3)]
        k = 0
        for s, t in PAIRS:
            for a in range(3):
                rows_s[pl.ds(first, 16), k, :] = place_parts[a][s]
                if own:
                    rows_t[pl.ds(first, 16), k, :] = -2.0 * place_parts[a][t]
                k += 1
        if own:
            shifted = split3(
                place[0] * place[0] + place[1] * place[1] + place[2] * place[2] + SOFTEN_NEAR
            )
        for s in range(3):
            rows_s[pl.ds(first, 16), k, :] = norm[s]
            if own:
                rows_t[pl.ds(first, 16), k, :] = one
            k += 1
        for s in range(3):
            rows_s[pl.ds(first, 16), k, :] = one
            if own:
                rows_t[pl.ds(first, 16), k, :] = shifted[s]
            k += 1
        for s, t in PAIRS[:3]:
            for ab in range(9):
                rows_s[pl.ds(first, 16), k, :] = outer[ab][s]
                if own:
                    rows_t[pl.ds(first, 16), k, :] = outer[ab][t]
                k += 1

    odd = [lax.axis_index(a) & 1 for a in AXES]
    upper = [CELLS + 2 * FACE * a + FACE * odd[a] for a in range(3)]
    lower = [CELLS + 2 * FACE * a + FACE * (1 - odd[a]) for a in range(3)]

    def arrange(c):
        block = rows_s[c]
        source[c] = block.astype(BF16).T
        points[c] = jnp.concatenate(
            [block[0:3], block[6:9], block[12:15], block[21:22], jnp.zeros((6, LANES), F32)],
            axis=0,
        ).astype(BF16)

    together = 8

    def faces_of(i):
        h, x = i & 1, i >> 1
        y_face = jnp.where(h == 0, lower[1], upper[1]) + 4 * x
        z_lower, z_upper = lower[2] + 2 * i, upper[2] + 2 * i
        return [y_face + k for k in range(4)] + [z_lower, z_lower + 1, z_upper, z_upper + 1]

    def first_own(k, carry):
        arrange(k)
        return carry

    def first_lower(k, carry):
        arrange(lower[0] + k)
        return carry

    lax.fori_loop(0, 24, first_own, 0, unroll=8)
    lax.fori_loop(0, FACE, first_lower, 0, unroll=8)
    for c in faces_of(0):
        arrange(c)
    row = lax.broadcasted_iota(jnp.int32, (DEPTH, LANES), 0)

    def step(i, carry):
        following = jnp.minimum(i + 1, CELLS // together - 1)
        ahead = jnp.where(
            following < 6, 8 * following + 16, upper[0] + 8 * (following & 1)
        )
        coming = [ahead + k for k in range(8)] + faces_of(following)
        weights = []
        spots = []
        for u in range(together):
            cell = i * together + u
            sources = source_index(cell, lower, upper)
            block = rows_t[cell]
            stationary = jnp.concatenate(
                [jnp.where(row < 24, block, 0.0), jnp.where(row < 24, 0.0, block)], axis=1
            ).astype(BF16)
            weights.append([])
            for k in range(7):
                pair = jnp.dot(source[sources[k]], stationary, preferred_element_type=F32)
                inverse = lax.rsqrt(pair[:, :LANES])
                weight = pair[:, LANES:] * (inverse * inverse * inverse)
                high = weight.astype(BF16)
                low = (weight - high.astype(F32)).astype(BF16)
                weights[u].append(jnp.concatenate([high, low], axis=1))
            spots.append([points[c] for c in sources])
            for c in coming[2 * u : 2 * u + 2]:
                arrange(c)
        for u in range(together):
            cell = i * together + u
            both = jnp.dot(
                jnp.concatenate(spots[u], axis=1),
                jnp.concatenate(weights[u], axis=0),
                preferred_element_type=F32,
            )
            sums = both[:, :LANES] + both[:, LANES:]
            moved = sums[0:3] + sums[3:6] + sums[6:9]
            base = rows_t[cell, 0:24, :]
            place = -0.5 * (base[0:3] + base[3:6] + base[9:12])
            near[cell] = place * sums[9:10] - moved
        return carry

    lax.fori_loop(0, CELLS // together, step, 0)


def force_kernel(
    gathered, near, masked, lines, stress, connect, node_pos, drag, values, second, first
):
    index_x, index_y, index_z = (lax.axis_index(a) for a in AXES)
    device = lax.broadcasted_iota(jnp.int32, (CELLS, 256), 1)
    cell = lax.broadcasted_iota(jnp.int32, (CELLS, 256), 0)
    gap = [
        (4 * index_x + cell // 16 - 4 * (device // 16)).astype(F32) - 0.5,
        (4 * index_y + (cell // 4) % 4 - 4 * ((device // 4) % 4)).astype(F32) - 0.5,
        (4 * index_z + cell % 4 - 4 * (device % 4)).astype(F32) - 0.5,
    ]
    square = [[gap[a] * gap[a], (gap[a] - 2.0) * (gap[a] - 2.0)] for a in range(3)]
    moments = gathered[...]
    lane = lax.broadcasted_iota(jnp.int32, (CELLS, LANES), 1)
    sigma = jnp.zeros((CELLS, LANES), F32)
    for sub in range(8):
        big_x, big_y, big_z = sub // 4, (sub // 2) % 2, sub % 2
        weight = lax.rsqrt(square[0][big_x] + square[1][big_y] + square[2][big_z] + SOFTEN_FAR)
        part = jnp.dot(
            weight, moments, precision=lax.Precision.HIGHEST, preferred_element_type=F32
        )
        sigma = jnp.where(lane // 16 == sub, part, sigma)
    for shift in (64, 32, 16):
        sigma = sigma + pltpu.roll(sigma, shift, 1)
    pull = [
        [FAR_SCALE * sigma[:, 3 * a + b : 3 * a + b + 1] + stress[a, b] for b in range(3)]
        for a in range(3)
    ]
    burger = [masked[a] for a in range(3)]
    line = [lines[a] for a in range(3)]
    pulled = [
        pull[a][0] * burger[0] + pull[a][1] * burger[1] + pull[a][2] * burger[2] for a in range(3)
    ]
    for a in range(3):
        b, c = (a + 1) % 3, (a + 2) % 3
        force = NEAR_SCALE * near[:, a, :] + (pulled[b] * line[c] - pulled[c] * line[b])
        high, rest = split2(0.5 * force)
        values[a] = high
        values[3 + a] = rest
    rows_high = lax.broadcasted_iota(jnp.int32, (8, LANES), 0)
    rows_low = lax.broadcasted_iota(jnp.int32, (LANES, LANES), 0)

    def scatter(i, total):
        left, right = [], []
        for u in range(STEP_CELLS):
            at = i * STEP_CELLS + u
            for end in range(2):
                node = connect[end, pl.ds(at, 1), :]
                high = node >> 7
                high = jnp.where(high < 4, high, high - 56)
                high = jnp.where((node < 512) | (node >= 7680), high, -1)
                chosen = rows_high == high
                left.append(
                    jnp.concatenate(
                        [jnp.where(chosen, values[q, pl.ds(at, 1), :], 0.0) for q in range(6)],
                        axis=0,
                    ).astype(BF16)
                )
                right.append((rows_low == (node & 127)).astype(F32).astype(BF16))
        return total + lax.dot_general(
            jnp.concatenate(left, axis=1),
            jnp.concatenate(right, axis=1),
            (((1,), (1,)), ((), ())),
            preferred_element_type=F32,
        )

    total = lax.fori_loop(0, CELLS // STEP_CELLS, scatter, jnp.zeros((48, LANES), F32))
    even = index_x % 2 == 0
    for a in range(3):
        force = total[8 * a : 8 * a + 8] + total[24 + 8 * a : 32 + 8 * a]
        slow = jnp.concatenate([drag[pl.ds(0, 4), :], drag[pl.ds(60, 4), :]], axis=0)
        place = jnp.concatenate([node_pos[a, pl.ds(0, 4), :], node_pos[a, pl.ds(60, 4), :]], axis=0)
        velocity = force / slow
        for row, field in ((a, place + TIME_STEP * velocity), (3 + a, velocity)):
            head, tail = field[0:4], field[4:8]
            first[row] = jnp.where(even, tail, head)
            second[row] = jnp.where(even, head, tail)


def node_kernel(values, connect, node_pos, drag, fields, sums):
    sums[...] = jnp.zeros(sums.shape, F32)
    rows_high = lax.broadcasted_iota(jnp.int32, (32, LANES), 0)
    rows_low = lax.broadcasted_iota(jnp.int32, (256, LANES), 0)

    def scatter(i, carry):
        left, right = [], []
        for u in range(STEP_CELLS):
            at = i * STEP_CELLS + u
            for end in range(2):
                node = connect[end, pl.ds(at, 1), :]
                chosen = rows_high == (node >> 8)
                left.append(
                    jnp.concatenate(
                        [jnp.where(chosen, values[q, pl.ds(at, 1), :], 0.0) for q in range(6)],
                        axis=0,
                    ).astype(BF16)
                )
                right.append((rows_low == (node & 255)).astype(F32).astype(BF16))
        sums[...] += lax.dot_general(
            jnp.concatenate(left, axis=1),
            jnp.concatenate(right, axis=1),
            (((1,), (1,)), ((), ())),
            preferred_element_type=F32,
        )
        return carry

    lax.fori_loop(0, CELLS // STEP_CELLS, scatter, 0, unroll=1)
    for a in range(3):
        force = sums[pl.ds(32 * a, 32), :] + sums[pl.ds(96 + 32 * a, 32), :]
        fields[3 + a, pl.ds(0, 32, stride=2), :] = force[:, :LANES]
        fields[3 + a, pl.ds(1, 32, stride=2), :] = force[:, LANES:]
    for a in range(3):
        velocity = fields[3 + a] / drag[...]
        fields[3 + a] = velocity
        fields[a] = node_pos[a] + TIME_STEP * velocity


def migrate_kernel(fields, first, second, shifts, out, joined):
    index_x, index_y, index_z = (lax.axis_index(a) for a in AXES)
    last = lax.axis_size("gx") - 1
    even = index_x % 2 == 0
    up_own = shifts[0, index_y, index_z, index_x]
    down_own = shifts[1, index_y, index_z, index_x]
    up_prev = jnp.where(
        index_x > 0, shifts[0, index_y, index_z, jnp.maximum(index_x - 1, 0)], 0
    )
    down_next = jnp.where(
        index_x < last, shifts[1, index_y, index_z, jnp.minimum(index_x + 1, last)], 0
    )
    kept = 8192 - up_own - down_own
    row = lax.broadcasted_iota(jnp.int32, (72, LANES), 0)
    lane = lax.broadcasted_iota(jnp.int32, (72, LANES), 1)
    position = row * LANES + lane
    pieces = (
        (512 - up_prev, position < up_prev),
        (512 + down_own - up_prev, position < up_prev + kept),
        (8704 - up_prev - kept, position < up_prev + kept + down_next),
    )
    for a in range(6):
        joined[pl.ds(0, 4), :] = jnp.where(even, second[a], first[a])
        joined[pl.ds(4, 64), :] = fields[a]
        joined[pl.ds(68, 4), :] = jnp.where(even, first[a], second[a])
        result = jnp.zeros((72, LANES), F32)
        for delta, within in reversed(pieces):
            rows, lanes = delta >> 7, delta & 127
            here = pltpu.roll(joined[pl.ds(rows, 72), :], (LANES - lanes) & 127, 1)
            after = pltpu.roll(joined[pl.ds(rows + 1, 72), :], (LANES - lanes) & 127, 1)
            moved = jnp.where(lane < LANES - lanes, here, after)
            result = jnp.where(within, moved, result)
        out[a] = result


def exchanged(array, axis, first):
    pairs = [(i, i + 1) for i in range(first, lax.axis_size(axis) - 1, 2)]
    return lax.ppermute(array, axis, pairs + [(b, a) for a, b in pairs])


def shape(*dims, dtype=F32):
    return pltpu.VMEM(dims, dtype)


def on_chip(array):
    return pltpu.with_memory_space_constraint(array, pltpu.VMEM)


def shards(offsets, burgers, lines, counts, connect, node_pos, drag, stress, shifts):
    offsets = offsets.reshape(3, CELLS, LANES)
    burgers = burgers.reshape(3, CELLS, LANES)
    lines = lines.reshape(3, CELLS, LANES)
    connect = connect.reshape(2, CELLS, LANES)
    node_pos = node_pos.reshape(3, 64, LANES)
    drag = drag.reshape(64, LANES)
    shifts = shifts.transpose(0, 2, 3, 1)
    vmem = pl.BlockSpec(memory_space=pltpu.VMEM)
    smem = pl.BlockSpec(memory_space=pltpu.SMEM)
    params = pltpu.CompilerParams(vmem_limit_bytes=VMEM)
    masked, moments, *sends = pl.pallas_call(
        prepare_kernel,
        in_specs=[vmem, vmem, vmem, smem],
        out_shape=[shape(3, CELLS, LANES), shape(256, LANES)] + [shape(9, FACE, LANES)] * 6,
        compiler_params=params,
        name="prepare",
    )(offsets, burgers, lines, counts)
    received = [None] * 6
    for i, send in zip(ORDER, sends):
        received[i] = exchanged(send, AXES[i // 2], i % 2)
    moments, *early = lax.optimization_barrier((moments, *[received[i] for i in ORDER[:5]]))
    for i, face in zip(ORDER, early):
        received[i] = face
    gathered = lax.all_to_all(
        moments.reshape(256, 1, LANES), AXES, 0, 0, tiled=True
    ).reshape(256, LANES)
    near = pl.pallas_call(
        near_kernel,
        in_specs=[vmem] * 9,
        out_shape=shape(CELLS, 3, LANES),
        scratch_shapes=[
            pltpu.VMEM((SOURCES, DEPTH, LANES), F32),
            pltpu.VMEM((CELLS, DEPTH, LANES), F32),
            pltpu.VMEM((SOURCES, LANES, DEPTH), BF16),
            pltpu.VMEM((SOURCES, 16, LANES), BF16),
        ],
        compiler_params=params,
        name="near",
    )(offsets, on_chip(masked), lines, *[on_chip(face) for face in received])
    values, *ends = pl.pallas_call(
        force_kernel,
        in_specs=[vmem] * 4 + [smem] + [vmem] * 3,
        out_shape=[shape(6, CELLS, LANES), shape(6, 4, LANES), shape(6, 4, LANES)],
        compiler_params=params,
        name="forces",
    )(on_chip(gathered), on_chip(near), on_chip(masked), lines, stress, connect, node_pos, drag)
    second = exchanged(ends[0], "gx", 1)
    first = exchanged(ends[1], "gx", 0)
    fields = pl.pallas_call(
        node_kernel,
        in_specs=[vmem] * 4,
        out_shape=shape(6, 64, LANES),
        scratch_shapes=[pltpu.VMEM((192, 256), F32)],
        compiler_params=params,
        name="nodes",
    )(on_chip(values), connect, node_pos, drag)
    out = pl.pallas_call(
        migrate_kernel,
        in_specs=[vmem] * 3 + [smem],
        out_shape=jax.ShapeDtypeStruct((6, 72, LANES), F32),
        scratch_shapes=[pltpu.VMEM((96, LANES), F32)],
        compiler_params=params,
        name="migrate",
    )(on_chip(fields), on_chip(first), on_chip(second), shifts)
    return out.reshape(6, 1, 1, 1, 72 * LANES)


def solution(mesh):
    cells = P(None, "gx", "gy", "gz", None)
    return jax.shard_map(
        shards,
        mesh=mesh,
        in_specs=(cells, cells, cells, P("gx", "gy", "gz"), cells, cells,
                  P("gx", "gy", "gz", None), P(), P()),
        out_specs=cells,
        check_vma=False,
    )
```

```python
import functools
import jax
import jax.numpy as jnp
from jax import lax
from jax.experimental import pallas as pl
from jax.experimental.pallas import tpu as pltpu
from jax.sharding import PartitionSpec as P

SOFTEN_NEAR = 0.25
SOFTEN_FAR = 4.0
NEAR_SCALE = 0.0625
FAR_SCALE = 0.03125
TIME_STEP = 0.1
AXES = ("gx", "gy", "gz")
F32 = jnp.float32
BF16 = jnp.bfloat16
LANES = 128
DEPTH = 64
STEP_CELLS = 16
ORDER = (1, 3, 5, 2, 4, 0)
CELLS = 64
FACE = 16
SOURCES = CELLS + 6 * FACE
VMEM = 60 << 20


def face_rows(axis):
    return (
        [(0, 48, 16, 1)],
        [(16 * x, 16 * x + 12, 4, 1) for x in range(4)],
        [(0, 3, 16, 4)],
    )[axis]


def split2(value):
    high = value.astype(BF16).astype(F32)
    return high, value - high


def split3(value):
    high = value.astype(BF16).astype(F32)
    rest = value - high
    middle = rest.astype(BF16).astype(F32)
    return high, middle, rest - middle


def prepare_kernel(offsets, burgers, lines, counts, masked, moments, *sends):
    slot = lax.broadcasted_iota(jnp.int32, (8, LANES), 1)
    row = lax.broadcasted_iota(jnp.int32, (8, LANES), 0)
    for group in range(8):
        live = jnp.zeros((8, LANES), jnp.int32)
        for s in range(8):
            cell = 8 * group + s
            live = jnp.where(row == s, counts[cell // 16, (cell // 4) % 4, cell % 4], live)
        for axis in range(3):
            block = burgers[axis, pl.ds(8 * group, 8), :]
            masked[axis, pl.ds(8 * group, 8), :] = jnp.where(slot < live, block, 0.0)
    sends = [sends[ORDER.index(i)] for i in range(6)]
    for axis in range(3):
        even = lax.axis_index(AXES[axis]) % 2 == 0
        to = 0
        for low, high, size, stride in face_rows(axis):
            at_low = pl.ds(low, size, stride=stride) if stride > 1 else pl.ds(low, size)
            at_high = pl.ds(high, size, stride=stride) if stride > 1 else pl.ds(high, size)
            for a in range(3):
                for part, array in enumerate((offsets, masked, lines)):
                    of_low, of_high = array[a, at_low, :], array[a, at_high, :]
                    sends[2 * axis][3 * part + a, pl.ds(to, size), :] = jnp.where(
                        even, of_high, of_low
                    )
                    sends[2 * axis + 1][3 * part + a, pl.ds(to, size), :] = jnp.where(
                        even, of_low, of_high
                    )
            to += size
    rows = []
    for coarse in range(4):
        big_x, big_y = coarse // 2, coarse % 2
        groups = (4 * big_x + big_y, 4 * big_x + 2 + big_y)
        for a in range(3):
            for b in range(3):
                rows.append(
                    sum(
                        masked[a, pl.ds(8 * g, 8), :] * lines[b, pl.ds(8 * g, 8), :]
                        for g in groups
                    )
                )
    stack = jnp.concatenate(rows, axis=0)
    ones = jnp.ones((8, 3 * LANES), F32).astype(BF16)
    summed = lax.dot_general(
        ones,
        jnp.concatenate(split3(stack), axis=1).astype(BF16),
        (((1,), (1,)), ((), ())),
        preferred_element_type=F32,
    )
    n = lax.broadcasted_iota(jnp.int32, (288, LANES), 0)
    lane = lax.broadcasted_iota(jnp.int32, (288, LANES), 1)
    target = ((n // 72) * 2 + (n % 4) // 2) * 16 + (n // 8) % 9
    pick = (lane == target).astype(F32).astype(BF16)
    packed = sum(
        jnp.dot(part.astype(BF16), pick, preferred_element_type=F32) for part in split3(summed)
    )
    moments[...] = jnp.broadcast_to(packed[0:1], moments.shape)


def source_index(target, lower, upper):
    x, y, z = target >> 4, (target >> 2) & 3, target & 3
    return [
        target,
        jnp.where(x > 0, target - 16, lower[0] + (target & 15)),
        jnp.where(x < 3, target + 16, upper[0] + (target & 15)),
        jnp.where(y > 0, target - 4, lower[1] + x * 4 + z),
        jnp.where(y < 3, target + 4, upper[1] + x * 4 + z),
        jnp.where(z > 0, target - 1, lower[2] + (target >> 2)),
        jnp.where(z < 3, target + 1, upper[2] + (target >> 2)),
    ]


PAIRS = ((0, 0), (0, 1), (1, 0), (0, 2), (2, 0), (1, 1))


def near_kernel(*refs):
    offsets, masked, lines = refs[:3]
    faces = refs[3:9]
    near = refs[9]
    rows_s, rows_t, source, points = refs[10:]
    blocks = []
    for first in range(0, CELLS, 16):
        cell = first + lax.broadcasted_iota(jnp.int32, (16, LANES), 0)
        corner = (cell // 16, (cell // 4) % 4, cell % 4)
        blocks.append(
            (
                first,
                [offsets[a, pl.ds(first, 16), :] + (corner[a].astype(F32) - 2.0) for a in range(3)],
                [masked[a, pl.ds(first, 16), :] for a in range(3)],
                [lines[a, pl.ds(first, 16), :] for a in range(3)],
            )
        )
    cell = lax.broadcasted_iota(jnp.int32, (16, LANES), 0)
    for f, face in enumerate(faces):
        fixed = f // 2
        others = [a for a in range(3) if a != fixed]
        corner = [None] * 3
        upper = lax.axis_index(AXES[fixed]) % 2 == f % 2
        corner[fixed] = jnp.where(upper, 2.0, -3.0).astype(F32)
        corner[others[0]] = (cell // 4).astype(F32) - 2.0
        corner[others[1]] = (cell % 4).astype(F32) - 2.0
        blocks.append(
            (
                CELLS + FACE * f,
                [face[a] + corner[a] for a in range(3)],
                [face[3 + a] for a in range(3)],
                [face[6 + a] for a in range(3)],
            )
        )
    one = jnp.ones((16, LANES), F32)
    rows_s[:, pl.ds(48, DEPTH - 48), :] = jnp.zeros((SOURCES, DEPTH - 48, LANES), F32)
    rows_t[:, pl.ds(48, DEPTH - 48), :] = jnp.zeros((CELLS, DEPTH - 48, LANES), F32)
    for first, place, burger, line in blocks:
        own = first < CELLS
        place_parts = [split3(p) for p in place]
        norm = split3(place[0] * place[0] + place[1] * place[1] + place[2] * place[2])
        outer = [split3(burger[a] * line[b]) for a in range(3) for b in range(3)]
        k = 0
        for s, t in PAIRS:
            for a in range(3):
                rows_s[pl.ds(first, 16), k, :] = place_parts[a][s]
                if own:
                    rows_t[pl.ds(first, 16), k, :] = -2.0 * place_parts[a][t]
                k += 1
        if own:
            shifted = split3(
                place[0] * place[0] + place[1] * place[1] + place[2] * place[2] + SOFTEN_NEAR
            )
        for s in range(3):
            rows_s[pl.ds(first, 16), k, :] = norm[s]
            if own:
                rows_t[pl.ds(first, 16), k, :] = one
            k += 1
        for s in range(3):
            rows_s[pl.ds(first, 16), k, :] = one
            if own:
                rows_t[pl.ds(first, 16), k, :] = shifted[s]
            k += 1
        for s, t in PAIRS[:3]:
            for ab in range(9):
                rows_s[pl.ds(first, 16), k, :] = outer[ab][s]
                if own:
                    rows_t[pl.ds(first, 16), k, :] = outer[ab][t]
                k += 1

    odd = [lax.axis_index(a) & 1 for a in AXES]
    upper = [CELLS + 2 * FACE * a + FACE * odd[a] for a in range(3)]
    lower = [CELLS + 2 * FACE * a + FACE * (1 - odd[a]) for a in range(3)]

    def arrange(c):
        block = rows_s[c]
        source[c] = block.astype(BF16).T
        points[c] = jnp.concatenate(
            [block[0:3], block[6:9], block[12:15], block[21:22], jnp.zeros((6, LANES), F32)],
            axis=0,
        ).astype(BF16)

    together = 8

    def faces_of(i):
        h, x = i & 1, i >> 1
        y_face = jnp.where(h == 0, lower[1], upper[1]) + 4 * x
        z_lower, z_upper = lower[2] + 2 * i, upper[2] + 2 * i
        return [y_face + k for k in range(4)] + [z_lower, z_lower + 1, z_upper, z_upper + 1]

    def first_own(k, carry):
        arrange(k)
        return carry

    def first_lower(k, carry):
        arrange(lower[0] + k)
        return carry

    lax.fori_loop(0, 24, first_own, 0, unroll=8)
    lax.fori_loop(0, FACE, first_lower, 0, unroll=8)
    for c in faces_of(0):
        arrange(c)
    row = lax.broadcasted_iota(jnp.int32, (DEPTH, LANES), 0)

    def step(i, carry):
        following = jnp.minimum(i + 1, CELLS // together - 1)
        ahead = jnp.where(
            following < 6, 8 * following + 16, upper[0] + 8 * (following & 1)
        )
        coming = [ahead + k for k in range(8)] + faces_of(following)
        weights = []
        spots = []
        for u in range(together):
            cell = i * together + u
            sources = source_index(cell, lower, upper)
            block = rows_t[cell]
            stationary = jnp.concatenate(
                [jnp.where(row < 24, block, 0.0), jnp.where(row < 24, 0.0, block)], axis=1
            ).astype(BF16)
            weights.append([])
            for k in range(7):
                pair = jnp.dot(source[sources[k]], stationary, preferred_element_type=F32)
                inverse = lax.rsqrt(pair[:, :LANES])
                weight = pair[:, LANES:] * (inverse * inverse * inverse)
                high = weight.astype(BF16)
                low = (weight - high.astype(F32)).astype(BF16)
                weights[u].append(jnp.concatenate([high, low], axis=1))
            spots.append([points[c] for c in sources])
            for c in coming[2 * u : 2 * u + 2]:
                arrange(c)
        for u in range(together):
            cell = i * together + u
            both = jnp.dot(
                jnp.concatenate(spots[u], axis=1),
                jnp.concatenate(weights[u], axis=0),
                preferred_element_type=F32,
            )
            sums = both[:, :LANES] + both[:, LANES:]
            moved = sums[0:3] + sums[3:6] + sums[6:9]
            base = rows_t[cell, 0:24, :]
            place = -0.5 * (base[0:3] + base[3:6] + base[9:12])
            near[cell] = place * sums[9:10] - moved
        return carry

    lax.fori_loop(0, CELLS // together, step, 0)


def force_kernel(
    gathered, near, masked, lines, stress, connect, node_pos, drag, values, second, first
):
    index_x, index_y, index_z = (lax.axis_index(a) for a in AXES)
    device = lax.broadcasted_iota(jnp.int32, (CELLS, 256), 1)
    cell = lax.broadcasted_iota(jnp.int32, (CELLS, 256), 0)
    gap = [
        (4 * index_x + cell // 16 - 4 * (device // 16)).astype(F32) - 0.5,
        (4 * index_y + (cell // 4) % 4 - 4 * ((device // 4) % 4)).astype(F32) - 0.5,
        (4 * index_z + cell % 4 - 4 * (device % 4)).astype(F32) - 0.5,
    ]
    square = [[gap[a] * gap[a], (gap[a] - 2.0) * (gap[a] - 2.0)] for a in range(3)]
    moments = gathered[...]
    lane = lax.broadcasted_iota(jnp.int32, (CELLS, LANES), 1)
    sigma = jnp.zeros((CELLS, LANES), F32)
    for sub in range(8):
        big_x, big_y, big_z = sub // 4, (sub // 2) % 2, sub % 2
        weight = lax.rsqrt(square[0][big_x] + square[1][big_y] + square[2][big_z] + SOFTEN_FAR)
        part = jnp.dot(
            weight, moments, precision=lax.Precision.HIGHEST, preferred_element_type=F32
        )
        sigma = jnp.where(lane // 16 == sub, part, sigma)
    for shift in (64, 32, 16):
        sigma = sigma + pltpu.roll(sigma, shift, 1)
    pull = [
        [FAR_SCALE * sigma[:, 3 * a + b : 3 * a + b + 1] + stress[a, b] for b in range(3)]
        for a in range(3)
    ]
    burger = [masked[a] for a in range(3)]
    line = [lines[a] for a in range(3)]
    pulled = [
        pull[a][0] * burger[0] + pull[a][1] * burger[1] + pull[a][2] * burger[2] for a in range(3)
    ]
    for a in range(3):
        b, c = (a + 1) % 3, (a + 2) % 3
        force = NEAR_SCALE * near[:, a, :] + (pulled[b] * line[c] - pulled[c] * line[b])
        high, rest = split2(0.5 * force)
        values[a] = high
        values[3 + a] = rest
    rows_high = lax.broadcasted_iota(jnp.int32, (8, LANES), 0)
    rows_low = lax.broadcasted_iota(jnp.int32, (LANES, LANES), 0)

    def scatter(i, total):
        left, right = [], []
        for u in range(STEP_CELLS):
            at = i * STEP_CELLS + u
            for end in range(2):
                node = connect[end, pl.ds(at, 1), :]
                high = node >> 7
                high = jnp.where(high < 4, high, high - 56)
                high = jnp.where((node < 512) | (node >= 7680), high, -1)
                chosen = rows_high == high
                left.append(
                    jnp.concatenate(
                        [jnp.where(chosen, values[q, pl.ds(at, 1), :], 0.0) for q in range(6)],
                        axis=0,
                    ).astype(BF16)
                )
                right.append((rows_low == (node & 127)).astype(F32).astype(BF16))
        return total + lax.dot_general(
            jnp.concatenate(left, axis=1),
            jnp.concatenate(right, axis=1),
            (((1,), (1,)), ((), ())),
            preferred_element_type=F32,
        )

    total = lax.fori_loop(0, CELLS // STEP_CELLS, scatter, jnp.zeros((48, LANES), F32))
    even = index_x % 2 == 0
    for a in range(3):
        force = total[8 * a : 8 * a + 8] + total[24 + 8 * a : 32 + 8 * a]
        slow = jnp.concatenate([drag[pl.ds(0, 4), :], drag[pl.ds(60, 4), :]], axis=0)
        place = jnp.concatenate([node_pos[a, pl.ds(0, 4), :], node_pos[a, pl.ds(60, 4), :]], axis=0)
        velocity = force / slow
        for row, field in ((a, place + TIME_STEP * velocity), (3 + a, velocity)):
            head, tail = field[0:4], field[4:8]
            first[row] = jnp.where(even, tail, head)
            second[row] = jnp.where(even, head, tail)


def node_kernel(values, connect, node_pos, drag, fields, sums):
    sums[...] = jnp.zeros(sums.shape, F32)
    rows_high = lax.broadcasted_iota(jnp.int32, (32, LANES), 0)
    rows_low = lax.broadcasted_iota(jnp.int32, (256, LANES), 0)

    def scatter(i, carry):
        left, right = [], []
        for u in range(STEP_CELLS):
            at = i * STEP_CELLS + u
            for end in range(2):
                node = connect[end, pl.ds(at, 1), :]
                chosen = rows_high == (node >> 8)
                left.append(
                    jnp.concatenate(
                        [jnp.where(chosen, values[q, pl.ds(at, 1), :], 0.0) for q in range(6)],
                        axis=0,
                    ).astype(BF16)
                )
                right.append((rows_low == (node & 255)).astype(F32).astype(BF16))
        sums[...] += lax.dot_general(
            jnp.concatenate(left, axis=1),
            jnp.concatenate(right, axis=1),
            (((1,), (1,)), ((), ())),
            preferred_element_type=F32,
        )
        return carry

    lax.fori_loop(0, CELLS // STEP_CELLS, scatter, 0, unroll=1)
    for a in range(3):
        force = sums[pl.ds(32 * a, 32), :] + sums[pl.ds(96 + 32 * a, 32), :]
        fields[3 + a, pl.ds(0, 32, stride=2), :] = force[:, :LANES]
        fields[3 + a, pl.ds(1, 32, stride=2), :] = force[:, LANES:]
    for a in range(3):
        velocity = fields[3 + a] / drag[...]
        fields[3 + a] = velocity
        fields[a] = node_pos[a] + TIME_STEP * velocity


def migrate_kernel(fields, first, second, shifts, out, joined):
    index_x, index_y, index_z = (lax.axis_index(a) for a in AXES)
    last = lax.axis_size("gx") - 1
    even = index_x % 2 == 0
    up_own = shifts[0, index_y, index_z, index_x]
    down_own = shifts[1, index_y, index_z, index_x]
    up_prev = jnp.where(
        index_x > 0, shifts[0, index_y, index_z, jnp.maximum(index_x - 1, 0)], 0
    )
    down_next = jnp.where(
        index_x < last, shifts[1, index_y, index_z, jnp.minimum(index_x + 1, last)], 0
    )
    kept = 8192 - up_own - down_own
    row = lax.broadcasted_iota(jnp.int32, (72, LANES), 0)
    lane = lax.broadcasted_iota(jnp.int32, (72, LANES), 1)
    position = row * LANES + lane
    pieces = (
        (512 - up_prev, position < up_prev),
        (512 + down_own - up_prev, position < up_prev + kept),
        (8704 - up_prev - kept, position < up_prev + kept + down_next),
    )
    for a in range(6):
        joined[pl.ds(0, 4), :] = jnp.where(even, second[a], first[a])
        joined[pl.ds(4, 64), :] = fields[a]
        joined[pl.ds(68, 4), :] = jnp.where(even, first[a], second[a])
        result = jnp.zeros((72, LANES), F32)
        for delta, within in reversed(pieces):
            rows, lanes = delta >> 7, delta & 127
            here = pltpu.roll(joined[pl.ds(rows, 72), :], (LANES - lanes) & 127, 1)
            after = pltpu.roll(joined[pl.ds(rows + 1, 72), :], (LANES - lanes) & 127, 1)
            moved = jnp.where(lane < LANES - lanes, here, after)
            result = jnp.where(within, moved, result)
        out[a] = result


def exchanged(array, axis, first):
    pairs = [(i, i + 1) for i in range(first, lax.axis_size(axis) - 1, 2)]
    return lax.ppermute(array, axis, pairs + [(b, a) for a, b in pairs])


def shape(*dims, dtype=F32):
    return pltpu.VMEM(dims, dtype)


def on_chip(array):
    return pltpu.with_memory_space_constraint(array, pltpu.VMEM)


def shards(offsets, burgers, lines, counts, connect, node_pos, drag, stress, shifts):
    offsets = offsets.reshape(3, CELLS, LANES)
    burgers = burgers.reshape(3, CELLS, LANES)
    lines = lines.reshape(3, CELLS, LANES)
    connect = connect.reshape(2, CELLS, LANES)
    node_pos = node_pos.reshape(3, 64, LANES)
    drag = drag.reshape(64, LANES)
    shifts = shifts.transpose(0, 2, 3, 1)
    vmem = pl.BlockSpec(memory_space=pltpu.VMEM)
    smem = pl.BlockSpec(memory_space=pltpu.SMEM)
    params = pltpu.CompilerParams(vmem_limit_bytes=VMEM)
    masked, moments, *sends = pl.pallas_call(
        prepare_kernel,
        in_specs=[vmem, vmem, vmem, smem],
        out_shape=[shape(3, CELLS, LANES), shape(256, LANES)] + [shape(9, FACE, LANES)] * 6,
        compiler_params=params,
        name="prepare",
    )(offsets, burgers, lines, counts)
    received = [None] * 6
    for i, send in zip(ORDER, sends):
        received[i] = exchanged(send, AXES[i // 2], i % 2)
    moments, *early = lax.optimization_barrier((moments, *[received[i] for i in ORDER[:5]]))
    for i, face in zip(ORDER, early):
        received[i] = face
    gathered = lax.all_to_all(
        moments.reshape(256, 1, LANES), AXES, 0, 0, tiled=True
    ).reshape(256, LANES)
    near = pl.pallas_call(
        near_kernel,
        in_specs=[vmem] * 9,
        out_shape=shape(CELLS, 3, LANES),
        scratch_shapes=[
            pltpu.VMEM((SOURCES, DEPTH, LANES), F32),
            pltpu.VMEM((CELLS, DEPTH, LANES), F32),
            pltpu.VMEM((SOURCES, LANES, DEPTH), BF16),
            pltpu.VMEM((SOURCES, 16, LANES), BF16),
        ],
        compiler_params=params,
        name="near",
    )(offsets, on_chip(masked), lines, *[on_chip(face) for face in received])
    values, *ends = pl.pallas_call(
        force_kernel,
        in_specs=[vmem] * 4 + [smem] + [vmem] * 3,
        out_shape=[shape(6, CELLS, LANES), shape(6, 4, LANES), shape(6, 4, LANES)],
        compiler_params=params,
        name="forces",
    )(on_chip(gathered), on_chip(near), on_chip(masked), lines, stress, connect, node_pos, drag)
    second = exchanged(ends[0], "gx", 1)
    first = exchanged(ends[1], "gx", 0)
    fields = pl.pallas_call(
        node_kernel,
        in_specs=[vmem] * 4,
        out_shape=shape(6, 64, LANES),
        scratch_shapes=[pltpu.VMEM((192, 256), F32)],
        compiler_params=params,
        name="nodes",
    )(on_chip(values), connect, node_pos, drag)
    out = pl.pallas_call(
        migrate_kernel,
        in_specs=[vmem] * 3 + [smem],
        out_shape=jax.ShapeDtypeStruct((6, 72, LANES), F32),
        scratch_shapes=[pltpu.VMEM((96, LANES), F32)],
        compiler_params=params,
        name="migrate",
    )(on_chip(fields), on_chip(first), on_chip(second), shifts)
    return out.reshape(6, 1, 1, 1, 72 * LANES)


def solution(mesh):
    cells = P(None, "gx", "gy", "gz", None)
    return jax.shard_map(
        shards,
        mesh=mesh,
        in_specs=(cells, cells, cells, P("gx", "gy", "gz"), cells, cells,
                  P("gx", "gy", "gz", None), P(), P()),
        out_specs=cells,
        check_vma=False,
    )
```

```python
import functools
import jax
import jax.numpy as jnp
from jax import lax
from jax.experimental import pallas as pl
from jax.experimental.pallas import tpu as pltpu
from jax.sharding import PartitionSpec as P

SOFTEN_NEAR = 0.25
SOFTEN_FAR = 4.0
NEAR_SCALE = 0.0625
FAR_SCALE = 0.03125
TIME_STEP = 0.1
AXES = ("gx", "gy", "gz")
F32 = jnp.float32
BF16 = jnp.bfloat16
LANES = 128
DEPTH = 64
STEP_CELLS = 16
ORDER = (1, 3, 5, 2, 4, 0)
CELLS = 64
FACE = 16
SOURCES = CELLS + 6 * FACE
VMEM = 60 << 20


def face_rows(axis):
    return (
        [(0, 48, 16, 1)],
        [(16 * x, 16 * x + 12, 4, 1) for x in range(4)],
        [(0, 3, 16, 4)],
    )[axis]


def split2(value):
    high = value.astype(BF16).astype(F32)
    return high, value - high


def split3(value):
    high = value.astype(BF16).astype(F32)
    rest = value - high
    middle = rest.astype(BF16).astype(F32)
    return high, middle, rest - middle


def prepare_kernel(offsets, burgers, lines, counts, masked, moments, *sends):
    slot = lax.broadcasted_iota(jnp.int32, (8, LANES), 1)
    row = lax.broadcasted_iota(jnp.int32, (8, LANES), 0)
    for group in range(8):
        live = jnp.zeros((8, LANES), jnp.int32)
        for s in range(8):
            cell = 8 * group + s
            live = jnp.where(row == s, counts[cell // 16, (cell // 4) % 4, cell % 4], live)
        for axis in range(3):
            block = burgers[axis, pl.ds(8 * group, 8), :]
            masked[axis, pl.ds(8 * group, 8), :] = jnp.where(slot < live, block, 0.0)
    sends = [sends[ORDER.index(i)] for i in range(6)]
    for axis in range(3):
        even = lax.axis_index(AXES[axis]) % 2 == 0
        to = 0
        for low, high, size, stride in face_rows(axis):
            at_low = pl.ds(low, size, stride=stride) if stride > 1 else pl.ds(low, size)
            at_high = pl.ds(high, size, stride=stride) if stride > 1 else pl.ds(high, size)
            for a in range(3):
                for part, array in enumerate((offsets, masked, lines)):
                    of_low, of_high = array[a, at_low, :], array[a, at_high, :]
                    sends[2 * axis][3 * part + a, pl.ds(to, size), :] = jnp.where(
                        even, of_high, of_low
                    )
                    sends[2 * axis + 1][3 * part + a, pl.ds(to, size), :] = jnp.where(
                        even, of_low, of_high
                    )
            to += size
    rows = []
    for coarse in range(4):
        big_x, big_y = coarse // 2, coarse % 2
        groups = (4 * big_x + big_y, 4 * big_x + 2 + big_y)
        for a in range(3):
            for b in range(3):
                rows.append(
                    sum(
                        masked[a, pl.ds(8 * g, 8), :] * lines[b, pl.ds(8 * g, 8), :]
                        for g in groups
                    )
                )
    stack = jnp.concatenate(rows, axis=0)
    ones = jnp.ones((8, 3 * LANES), F32).astype(BF16)
    summed = lax.dot_general(
        ones,
        jnp.concatenate(split3(stack), axis=1).astype(BF16),
        (((1,), (1,)), ((), ())),
        preferred_element_type=F32,
    )
    n = lax.broadcasted_iota(jnp.int32, (288, LANES), 0)
    lane = lax.broadcasted_iota(jnp.int32, (288, LANES), 1)
    target = ((n // 72) * 2 + (n % 4) // 2) * 16 + (n // 8) % 9
    pick = (lane == target).astype(F32).astype(BF16)
    packed = sum(
        jnp.dot(part.astype(BF16), pick, preferred_element_type=F32) for part in split3(summed)
    )
    moments[...] = jnp.broadcast_to(packed[0:1], moments.shape)


def source_index(target, lower, upper):
    x, y, z = target >> 4, (target >> 2) & 3, target & 3
    return [
        target,
        jnp.where(x > 0, target - 16, lower[0] + (target & 15)),
        jnp.where(x < 3, target + 16, upper[0] + (target & 15)),
        jnp.where(y > 0, target - 4, lower[1] + x * 4 + z),
        jnp.where(y < 3, target + 4, upper[1] + x * 4 + z),
        jnp.where(z > 0, target - 1, lower[2] + (target >> 2)),
        jnp.where(z < 3, target + 1, upper[2] + (target >> 2)),
    ]


PAIRS = ((0, 0), (0, 1), (1, 0), (0, 2), (2, 0), (1, 1))


def near_kernel(*refs):
    offsets, masked, lines = refs[:3]
    faces = refs[3:9]
    near = refs[9]
    rows_s, rows_t, source, points = refs[10:]
    blocks = []
    for first in range(0, CELLS, 16):
        cell = first + lax.broadcasted_iota(jnp.int32, (16, LANES), 0)
        corner = (cell // 16, (cell // 4) % 4, cell % 4)
        blocks.append(
            (
                first,
                [offsets[a, pl.ds(first, 16), :] + (corner[a].astype(F32) - 2.0) for a in range(3)],
                [masked[a, pl.ds(first, 16), :] for a in range(3)],
                [lines[a, pl.ds(first, 16), :] for a in range(3)],
            )
        )
    cell = lax.broadcasted_iota(jnp.int32, (16, LANES), 0)
    for f, face in enumerate(faces):
        fixed = f // 2
        others = [a for a in range(3) if a != fixed]
        corner = [None] * 3
        upper = lax.axis_index(AXES[fixed]) % 2 == f % 2
        corner[fixed] = jnp.where(upper, 2.0, -3.0).astype(F32)
        corner[others[0]] = (cell // 4).astype(F32) - 2.0
        corner[others[1]] = (cell % 4).astype(F32) - 2.0
        blocks.append(
            (
                CELLS + FACE * f,
                [face[a] + corner[a] for a in range(3)],
                [face[3 + a] for a in range(3)],
                [face[6 + a] for a in range(3)],
            )
        )
    one = jnp.ones((16, LANES), F32)
    rows_s[:, pl.ds(48, DEPTH - 48), :] = jnp.zeros((SOURCES, DEPTH - 48, LANES), F32)
    rows_t[:, pl.ds(48, DEPTH - 48), :] = jnp.zeros((CELLS, DEPTH - 48, LANES), F32)
    for first, place, burger, line in blocks:
        own = first < CELLS
        place_parts = [split3(p) for p in place]
        norm = split3(place[0] * place[0] + place[1] * place[1] + place[2] * place[2])
        outer = [split3(burger[a] * line[b]) for a in range(3) for b in range(3)]
        k = 0
        for s, t in PAIRS:
            for a in range(3):
                rows_s[pl.ds(first, 16), k, :] = place_parts[a][s]
                if own:
                    rows_t[pl.ds(first, 16), k, :] = -2.0 * place_parts[a][t]
                k += 1
        if own:
            shifted = split3(
                place[0] * place[0] + place[1] * place[1] + place[2] * place[2] + SOFTEN_NEAR
            )
        for s in range(3):
            rows_s[pl.ds(first, 16), k, :] = norm[s]
            if own:
                rows_t[pl.ds(first, 16), k, :] = one
            k += 1
        for s in range(3):
            rows_s[pl.ds(first, 16), k, :] = one
            if own:
                rows_t[pl.ds(first, 16), k, :] = shifted[s]
            k += 1
        for s, t in PAIRS[:3]:
            for ab in range(9):
                rows_s[pl.ds(first, 16), k, :] = outer[ab][s]
                if own:
                    rows_t[pl.ds(first, 16), k, :] = outer[ab][t]
                k += 1

    odd = [lax.axis_index(a) & 1 for a in AXES]
    upper = [CELLS + 2 * FACE * a + FACE * odd[a] for a in range(3)]
    lower = [CELLS + 2 * FACE * a + FACE * (1 - odd[a]) for a in range(3)]

    def arrange(c):
        block = rows_s[c]
        source[c] = block.astype(BF16).T
        points[c] = jnp.concatenate(
            [block[0:3], block[6:9], block[12:15], block[21:22], jnp.zeros((6, LANES), F32)],
            axis=0,
        ).astype(BF16)

    together = 8

    def faces_of(i):
        h, x = i & 1, i >> 1
        y_face = jnp.where(h == 0, lower[1], upper[1]) + 4 * x
        z_lower, z_upper = lower[2] + 2 * i, upper[2] + 2 * i
        return [y_face + k for k in range(4)] + [z_lower, z_lower + 1, z_upper, z_upper + 1]

    def first_own(k, carry):
        arrange(k)
        return carry

    def first_lower(k, carry):
        arrange(lower[0] + k)
        return carry

    lax.fori_loop(0, 24, first_own, 0, unroll=8)
    lax.fori_loop(0, FACE, first_lower, 0, unroll=8)
    for c in faces_of(0):
        arrange(c)
    row = lax.broadcasted_iota(jnp.int32, (DEPTH, LANES), 0)

    def step(i, carry):
        following = jnp.minimum(i + 1, CELLS // together - 1)
        ahead = jnp.where(
            following < 6, 8 * following + 16, upper[0] + 8 * (following & 1)
        )
        coming = [ahead + k for k in range(8)] + faces_of(following)
        weights = []
        spots = []
        for u in range(together):
            cell = i * together + u
            sources = source_index(cell, lower, upper)
            block = rows_t[cell]
            stationary = jnp.concatenate(
                [jnp.where(row < 24, block, 0.0), jnp.where(row < 24, 0.0, block)], axis=1
            ).astype(BF16)
            weights.append([])
            for k in range(7):
                pair = jnp.dot(source[sources[k]], stationary, preferred_element_type=F32)
                inverse = lax.rsqrt(pair[:, :LANES])
                weight = pair[:, LANES:] * (inverse * inverse * inverse)
                high = weight.astype(BF16)
                low = (weight - high.astype(F32)).astype(BF16)
                weights[u].append(jnp.concatenate([high, low], axis=1))
            spots.append([points[c] for c in sources])
            for c in coming[2 * u : 2 * u + 2]:
                arrange(c)
        for u in range(together):
            cell = i * together + u
            both = jnp.dot(
                jnp.concatenate(spots[u], axis=1),
                jnp.concatenate(weights[u], axis=0),
                preferred_element_type=F32,
            )
            sums = both[:, :LANES] + both[:, LANES:]
            moved = sums[0:3] + sums[3:6] + sums[6:9]
            base = rows_t[cell, 0:24, :]
            place = -0.5 * (base[0:3] + base[3:6] + base[9:12])
            near[cell] = place * sums[9:10] - moved
        return carry

    lax.fori_loop(0, CELLS // together, step, 0)


def force_kernel(
    gathered, near, masked, lines, stress, connect, node_pos, drag, values, second, first
):
    index_x, index_y, index_z = (lax.axis_index(a) for a in AXES)
    device = lax.broadcasted_iota(jnp.int32, (CELLS, 256), 1)
    cell = lax.broadcasted_iota(jnp.int32, (CELLS, 256), 0)
    gap = [
        (4 * index_x + cell // 16 - 4 * (device // 16)).astype(F32) - 0.5,
        (4 * index_y + (cell // 4) % 4 - 4 * ((device // 4) % 4)).astype(F32) - 0.5,
        (4 * index_z + cell % 4 - 4 * (device % 4)).astype(F32) - 0.5,
    ]
    square = [[gap[a] * gap[a], (gap[a] - 2.0) * (gap[a] - 2.0)] for a in range(3)]
    moments = gathered[...]
    lane = lax.broadcasted_iota(jnp.int32, (CELLS, LANES), 1)
    sigma = jnp.zeros((CELLS, LANES), F32)
    for sub in range(8):
        big_x, big_y, big_z = sub // 4, (sub // 2) % 2, sub % 2
        weight = lax.rsqrt(square[0][big_x] + square[1][big_y] + square[2][big_z] + SOFTEN_FAR)
        part = jnp.dot(
            weight, moments, precision=lax.Precision.HIGHEST, preferred_element_type=F32
        )
        sigma = jnp.where(lane // 16 == sub, part, sigma)
    for shift in (64, 32, 16):
        sigma = sigma + pltpu.roll(sigma, shift, 1)
    pull = [
        [FAR_SCALE * sigma[:, 3 * a + b : 3 * a + b + 1] + stress[a, b] for b in range(3)]
        for a in range(3)
    ]
    burger = [masked[a] for a in range(3)]
    line = [lines[a] for a in range(3)]
    pulled = [
        pull[a][0] * burger[0] + pull[a][1] * burger[1] + pull[a][2] * burger[2] for a in range(3)
    ]
    for a in range(3):
        b, c = (a + 1) % 3, (a + 2) % 3
        force = NEAR_SCALE * near[:, a, :] + (pulled[b] * line[c] - pulled[c] * line[b])
        high, rest = split2(0.5 * force)
        values[a] = high
        values[3 + a] = rest
    rows_high = lax.broadcasted_iota(jnp.int32, (8, LANES), 0)
    rows_low = lax.broadcasted_iota(jnp.int32, (LANES, LANES), 0)

    def scatter(i, total):
        left, right = [], []
        for u in range(STEP_CELLS):
            at = i * STEP_CELLS + u
            for end in range(2):
                node = connect[end, pl.ds(at, 1), :]
                high = node >> 7
                high = jnp.where(high < 4, high, high - 56)
                high = jnp.where((node < 512) | (node >= 7680), high, -1)
                chosen = rows_high == high
                left.append(
                    jnp.concatenate(
                        [jnp.where(chosen, values[q, pl.ds(at, 1), :], 0.0) for q in range(6)],
                        axis=0,
                    ).astype(BF16)
                )
                right.append((rows_low == (node & 127)).astype(F32).astype(BF16))
        return total + lax.dot_general(
            jnp.concatenate(left, axis=1),
            jnp.concatenate(right, axis=1),
            (((1,), (1,)), ((), ())),
            preferred_element_type=F32,
        )

    total = lax.fori_loop(0, CELLS // STEP_CELLS, scatter, jnp.zeros((48, LANES), F32), unroll=2)
    even = index_x % 2 == 0
    for a in range(3):
        force = total[8 * a : 8 * a + 8] + total[24 + 8 * a : 32 + 8 * a]
        slow = jnp.concatenate([drag[pl.ds(0, 4), :], drag[pl.ds(60, 4), :]], axis=0)
        place = jnp.concatenate([node_pos[a, pl.ds(0, 4), :], node_pos[a, pl.ds(60, 4), :]], axis=0)
        velocity = force / slow
        for row, field in ((a, place + TIME_STEP * velocity), (3 + a, velocity)):
            head, tail = field[0:4], field[4:8]
            first[row] = jnp.where(even, tail, head)
            second[row] = jnp.where(even, head, tail)


def node_kernel(values, connect, node_pos, drag, fields, sums):
    sums[...] = jnp.zeros(sums.shape, F32)
    rows_high = lax.broadcasted_iota(jnp.int32, (32, LANES), 0)
    rows_low = lax.broadcasted_iota(jnp.int32, (256, LANES), 0)

    def scatter(i, carry):
        left, right = [], []
        for u in range(STEP_CELLS):
            at = i * STEP_CELLS + u
            for end in range(2):
                node = connect[end, pl.ds(at, 1), :]
                chosen = rows_high == (node >> 8)
                left.append(
                    jnp.concatenate(
                        [jnp.where(chosen, values[q, pl.ds(at, 1), :], 0.0) for q in range(6)],
                        axis=0,
                    ).astype(BF16)
                )
                right.append((rows_low == (node & 255)).astype(F32).astype(BF16))
        sums[...] += lax.dot_general(
            jnp.concatenate(left, axis=1),
            jnp.concatenate(right, axis=1),
            (((1,), (1,)), ((), ())),
            preferred_element_type=F32,
        )
        return carry

    lax.fori_loop(0, CELLS // STEP_CELLS, scatter, 0, unroll=2)
    for a in range(3):
        force = sums[pl.ds(32 * a, 32), :] + sums[pl.ds(96 + 32 * a, 32), :]
        fields[3 + a, pl.ds(0, 32, stride=2), :] = force[:, :LANES]
        fields[3 + a, pl.ds(1, 32, stride=2), :] = force[:, LANES:]
    for a in range(3):
        velocity = fields[3 + a] / drag[...]
        fields[3 + a] = velocity
        fields[a] = node_pos[a] + TIME_STEP * velocity


def migrate_kernel(fields, first, second, shifts, out, joined):
    index_x, index_y, index_z = (lax.axis_index(a) for a in AXES)
    last = lax.axis_size("gx") - 1
    even = index_x % 2 == 0
    up_own = shifts[0, index_y, index_z, index_x]
    down_own = shifts[1, index_y, index_z, index_x]
    up_prev = jnp.where(
        index_x > 0, shifts[0, index_y, index_z, jnp.maximum(index_x - 1, 0)], 0
    )
    down_next = jnp.where(
        index_x < last, shifts[1, index_y, index_z, jnp.minimum(index_x + 1, last)], 0
    )
    kept = 8192 - up_own - down_own
    row = lax.broadcasted_iota(jnp.int32, (72, LANES), 0)
    lane = lax.broadcasted_iota(jnp.int32, (72, LANES), 1)
    position = row * LANES + lane
    pieces = (
        (512 - up_prev, position < up_prev),
        (512 + down_own - up_prev, position < up_prev + kept),
        (8704 - up_prev - kept, position < up_prev + kept + down_next),
    )
    for a in range(6):
        joined[pl.ds(0, 4), :] = jnp.where(even, second[a], first[a])
        joined[pl.ds(4, 64), :] = fields[a]
        joined[pl.ds(68, 4), :] = jnp.where(even, first[a], second[a])
        result = jnp.zeros((72, LANES), F32)
        for delta, within in reversed(pieces):
            rows, lanes = delta >> 7, delta & 127
            here = pltpu.roll(joined[pl.ds(rows, 72), :], (LANES - lanes) & 127, 1)
            after = pltpu.roll(joined[pl.ds(rows + 1, 72), :], (LANES - lanes) & 127, 1)
            moved = jnp.where(lane < LANES - lanes, here, after)
            result = jnp.where(within, moved, result)
        out[a] = result


def exchanged(array, axis, first):
    pairs = [(i, i + 1) for i in range(first, lax.axis_size(axis) - 1, 2)]
    return lax.ppermute(array, axis, pairs + [(b, a) for a, b in pairs])


def shape(*dims, dtype=F32):
    return pltpu.VMEM(dims, dtype)


def on_chip(array):
    return pltpu.with_memory_space_constraint(array, pltpu.VMEM)


def shards(offsets, burgers, lines, counts, connect, node_pos, drag, stress, shifts):
    offsets = offsets.reshape(3, CELLS, LANES)
    burgers = burgers.reshape(3, CELLS, LANES)
    lines = lines.reshape(3, CELLS, LANES)
    connect = connect.reshape(2, CELLS, LANES)
    node_pos = node_pos.reshape(3, 64, LANES)
    drag = drag.reshape(64, LANES)
    shifts = shifts.transpose(0, 2, 3, 1)
    vmem = pl.BlockSpec(memory_space=pltpu.VMEM)
    smem = pl.BlockSpec(memory_space=pltpu.SMEM)
    params = pltpu.CompilerParams(vmem_limit_bytes=VMEM)
    masked, moments, *sends = pl.pallas_call(
        prepare_kernel,
        in_specs=[vmem, vmem, vmem, smem],
        out_shape=[shape(3, CELLS, LANES), shape(256, LANES)] + [shape(9, FACE, LANES)] * 6,
        compiler_params=params,
        name="prepare",
    )(offsets, burgers, lines, counts)
    received = [None] * 6
    for i, send in zip(ORDER, sends):
        received[i] = exchanged(send, AXES[i // 2], i % 2)
    moments, *early = lax.optimization_barrier((moments, *[received[i] for i in ORDER[:5]]))
    for i, face in zip(ORDER, early):
        received[i] = face
    gathered = lax.all_to_all(
        moments.reshape(256, 1, LANES), AXES, 0, 0, tiled=True
    ).reshape(256, LANES)
    near = pl.pallas_call(
        near_kernel,
        in_specs=[vmem] * 9,
        out_shape=shape(CELLS, 3, LANES),
        scratch_shapes=[
            pltpu.VMEM((SOURCES, DEPTH, LANES), F32),
            pltpu.VMEM((CELLS, DEPTH, LANES), F32),
            pltpu.VMEM((SOURCES, LANES, DEPTH), BF16),
            pltpu.VMEM((SOURCES, 16, LANES), BF16),
        ],
        compiler_params=params,
        name="near",
    )(offsets, on_chip(masked), lines, *[on_chip(face) for face in received])
    values, *ends = pl.pallas_call(
        force_kernel,
        in_specs=[vmem] * 4 + [smem] + [vmem] * 3,
        out_shape=[shape(6, CELLS, LANES), shape(6, 4, LANES), shape(6, 4, LANES)],
        compiler_params=params,
        name="forces",
    )(on_chip(gathered), on_chip(near), on_chip(masked), lines, stress, connect, node_pos, drag)
    second = exchanged(ends[0], "gx", 1)
    first = exchanged(ends[1], "gx", 0)
    fields = pl.pallas_call(
        node_kernel,
        in_specs=[vmem] * 4,
        out_shape=shape(6, 64, LANES),
        scratch_shapes=[pltpu.VMEM((192, 256), F32)],
        compiler_params=params,
        name="nodes",
    )(on_chip(values), connect, node_pos, drag)
    out = pl.pallas_call(
        migrate_kernel,
        in_specs=[vmem] * 3 + [smem],
        out_shape=jax.ShapeDtypeStruct((6, 72, LANES), F32),
        scratch_shapes=[pltpu.VMEM((96, LANES), F32)],
        compiler_params=params,
        name="migrate",
    )(on_chip(fields), on_chip(first), on_chip(second), shifts)
    return out.reshape(6, 1, 1, 1, 72 * LANES)


def solution(mesh):
    cells = P(None, "gx", "gy", "gz", None)
    return jax.shard_map(
        shards,
        mesh=mesh,
        in_specs=(cells, cells, cells, P("gx", "gy", "gz"), cells, cells,
                  P("gx", "gy", "gz", None), P(), P()),
        out_specs=cells,
        check_vma=False,
    )
```
